512 devices in a mesh: req: 128 (over z, y, core), rep: 4 (over x).
Axes of the slice: x: 4, y: 8, z: 8, core: 2. Of those that a mesh axis runs over, the one named last changes fastest.
Arguments:
- prefill_qkv: bfloat16 [65536, 3, 1792], P(('rep', 'req')), parts along dimension 0, may hold values from -6 to 6
- decode_qkv: bfloat16 [4096, 3, 1792], P(('rep', 'req')), parts along dimension 0, may hold values from -6 to 6
- conv_state: bfloat16 [4608, 2, 1792], P(('rep', 'req')), parts along dimension 0, may hold values from -6 to 6
- cache_len: int32 [4608], P(('rep', 'req')), parts along dimension 0, may hold values from 0 to 32768, as said below
- page_table: int32 [4608, 256], P(('rep', 'req')), parts along dimension 0, may hold values from 0 to 1
- page_pool: bfloat16 [1024, 2, 128, 1792], P(('rep', 'req')), parts along dimension 0, may hold values from -6 to 6
- conv_taps: float32 [3, 1792], replicated, may hold values from -3.5 to 3.5
- segment_owner: int32 [512], P('rep'), parts along dimension 0, may hold values from 0 to 127, each once
- regroup: int32 [69632], P('rep'), parts along dimension 0, may hold values from 0 to 17407, as said below
- residual: bfloat16 [69632, 1792], P(('rep', 'req')), parts along dimension 0, may hold values from -4 to 4
- norm_gain: float32 [1792], replicated, may hold values from 0.5 to 1.5
Outputs:
- new_residual: bfloat16 [69632, 1792], P(('rep', 'req')), parts along dimension 0
- normed: bfloat16 [69632, 1792], P(('rep', 'req')), parts along dimension 0
The draws below stay inside these ranges and needn't reach their ends.
There are 4 independent parts, one for each index of `rep`. The reference program is written for one: setup_inputs(seed, part) draws one part's arguments, and reference() takes and returns one part's arrays. A program takes and returns all parts, laid end to end along the dimension named above; an argument that names none is the same for every part. Nothing has to cross between parts.
Inputs may be any that keep to these rules, and one draw needn't show every extreme that they name: `cache_len`: some request holds exactly 32768 cached positions. `page_table`: page numbers index the serving device's own 2 pages. `segment_owner`: A permutation of the devices: every device serves exactly one segment. `regroup`: A permutation: live row g goes to device (g + R) mod 128 for one drawn R, so every device receives 136 rows, and at most 2 rows go from one device to one device, a bound that every device reaches.
All inputs are finite; a program needn't handle non-finite values.
Results may differ from the reference program's by a relative error of at most 0.0052.
Values may be sent and summed in bfloat16 or wider, within the bound.
A program may use at most 128 MiB of HBM per device.

```python
import jax
import jax.numpy as jnp
from jax import lax

D = 1792
HEADS = 16
HEAD_CHANNELS = 112
WINDOW = 64
TAPS = 3
PAGE = 128
MAX_CACHE = 32768
MAX_PAGES = 256
POOL_DEV = 2
SEGMENT = 128
DEC_DEV = 8
REQ_DEV = 9
SEGMENTS = 128
TOK_DEV = 136
LIVE = 17408
N_REQ = 128


def draw_cache_len(key, part):
    request_count = N_REQ * REQ_DEV
    key_long, key_short, key_pick, key_chosen = jax.random.split(jax.random.fold_in(key, 11), 4)
    longer = jax.random.randint(key_long, (request_count,), 0, MAX_CACHE + 1)
    shorter = jax.random.randint(key_short, (request_count,), 0, 2 * WINDOW)
    picker = jax.random.randint(key_pick, (request_count,), 0, 4)
    lengths = jnp.where(picker == 0, shorter, longer)
    chosen = jax.random.randint(key_chosen, (), 0, request_count)
    return lengths.at[chosen].set(MAX_CACHE).astype(jnp.int32)


def draw_regroup(key, part):
    key_rotation, key_offsets = jax.random.split(jax.random.fold_in(key, 23))
    rotation = jax.random.randint(key_rotation, (), 0, N_REQ)
    offsets = jax.random.randint(key_offsets, (N_REQ,), 0, TOK_DEV)
    shifted = jnp.arange(LIVE, dtype=jnp.int32) + rotation
    target = shifted % N_REQ
    slot_index = (shifted // N_REQ + offsets[target]) % TOK_DEV
    return (target * TOK_DEV + slot_index).astype(jnp.int32)


def plant(drawn, stream_key, least, high):
    dims = drawn.shape
    place = [jax.random.randint(jax.random.fold_in(stream_key, axis), (), 0, dims[axis]) for axis in range(len(dims))]
    drawn = drawn.at[tuple(place)].set(least)
    longest = dims.index(max(dims))
    place[longest] = (place[longest] + 1) % dims[longest]
    return drawn.at[tuple(place)].set(high)


def steps_of(stream_key, shape, cuts, low, high):
    def one(dim, blocks):
        steps = jax.random.uniform(jax.random.fold_in(jax.random.fold_in(stream_key, 6), dim), (blocks,), jnp.float32, low / len(cuts), high / len(cuts))
        return jnp.repeat(jnp.exp(steps), shape[dim] // blocks).reshape((-1,) + (1,) * (len(shape) - dim - 1))

    factor_of = one(*cuts[0])
    for cut in cuts[1:]:
        factor_of = factor_of * one(*cut)
    return factor_of


def noise(key, extent, deviation, reach, pieces=(), held_as=jnp.bfloat16):
    values = deviation * jax.random.normal(key, extent, jnp.float32)
    if pieces:
        values = values * steps_of(key, extent, pieces, -0.22, 0.18)
    return jnp.clip(values, -reach, reach).astype(held_as)


def setup_inputs(seed: int = 0, part: int = 0) -> dict:
    seeds = jax.random.split(jax.random.key(seed), 12)
    part_splits = jax.random.split(jax.random.fold_in(seeds[11], part), 12)
    return {
        "prefill_qkv": noise(part_splits[0], (N_REQ * SEGMENT, 3, D), 1.0, 6.0, ((0, 128),)),
        "decode_qkv": noise(part_splits[1], (N_REQ * DEC_DEV, 3, D), 1.0, 6.0, ((0, 128),)),
        "conv_state": noise(part_splits[2], (N_REQ * REQ_DEV, 2, D), 1.0, 6.0, ((0, 128),)),
        "cache_len": draw_cache_len(jax.random.fold_in(jax.random.fold_in(seeds[11], part), 71), part),
        "page_table": plant(jax.random.randint(part_splits[4], (N_REQ * REQ_DEV, MAX_PAGES), 0, POOL_DEV), jax.random.fold_in(part_splits[4], 1), 0, POOL_DEV - 1).astype(jnp.int32),
        "page_pool": noise(part_splits[5], (N_REQ * POOL_DEV, 2, PAGE, D), 1.0, 6.0, ((0, 128),)),
        "conv_taps": noise(seeds[6], (TAPS, D), TAPS ** -0.5, 3.5, (), jnp.float32),
        "segment_owner": jax.random.permutation(part_splits[7], N_REQ).astype(jnp.int32),
        "regroup": draw_regroup(jax.random.fold_in(jax.random.fold_in(seeds[11], part), 71), part),
        "residual": noise(part_splits[9], (LIVE, D), 0.5, 4.0, ((0, 128),)),
        "norm_gain": jnp.clip(1.0 + 0.1 * jax.random.normal(seeds[10], (D,), jnp.float32), 0.5, 1.5),
    }


norm_eps = 1e-06
masked_score = -1e+30

def short_conv(conv_tail, raw_keys, conv_taps):
    extended = jnp.concatenate([conv_tail, raw_keys], axis=0).astype(jnp.float32)
    length = raw_keys.shape[0]
    convolved = conv_taps[0] * extended[0:length] + conv_taps[1] * extended[1:length + 1] + conv_taps[2] * extended[2:length + 2]
    return convolved.astype(jnp.bfloat16)

def cache_rows(pool_dev, table_row, cached):
    positions = cached - (WINDOW - 1) + jnp.arange(WINDOW - 1, dtype=jnp.int32)
    usable = positions >= 0
    clipped = jnp.maximum(positions, 0)
    physical = table_row[clipped // PAGE]
    offsets = clipped % PAGE
    return (pool_dev[physical, 0, offsets], pool_dev[physical, 1, offsets], positions, usable)

def attend(queries, key_rows, value_rows, query_pos, key_pos, usable):
    length = queries.shape[0]
    span = key_rows.shape[0]
    query_head_rows = queries.reshape(length, HEADS, HEAD_CHANNELS).astype(jnp.float32)
    key_head_rows = key_rows.reshape(span, HEADS, HEAD_CHANNELS).astype(jnp.float32)
    value_head_rows = value_rows.reshape(span, HEADS, HEAD_CHANNELS).astype(jnp.float32)
    logit_scores = jnp.einsum('wps,aps->pwa', query_head_rows, key_head_rows) * HEAD_CHANNELS ** (-0.5)
    allowed = usable[None, :] & (key_pos[None, :] <= query_pos[:, None]) & (key_pos[None, :] >= query_pos[:, None] - (WINDOW - 1))
    logit_scores = jnp.where(allowed[None], logit_scores, masked_score)
    row_max = lax.optimization_barrier(jnp.max(logit_scores, axis=2, keepdims=True))
    raised = jnp.exp(logit_scores - row_max)
    softmax_weights = (raised / lax.optimization_barrier(jnp.sum(raised, axis=2, keepdims=True))).astype(jnp.bfloat16)
    attended_output = jnp.einsum('wks,swp->kwp', softmax_weights.astype(jnp.float32), value_head_rows)
    return attended_output.reshape(length, HEADS * HEAD_CHANNELS).astype(jnp.bfloat16)

def request_context(triple, conv_tail, cached, table_row, pool_dev, conv_taps):
    length = triple.shape[0]
    fresh_keys = short_conv(conv_tail, triple[:, 1], conv_taps)
    cache_keys, cache_values, cache_pos, cache_ok = cache_rows(pool_dev, table_row, cached)
    key_rows = jnp.concatenate([cache_keys, fresh_keys], axis=0)
    value_rows = jnp.concatenate([cache_values, triple[:, 2]], axis=0)
    fresh_pos = cached + jnp.arange(length, dtype=jnp.int32)
    key_pos = jnp.concatenate([cache_pos, fresh_pos], axis=0)
    usable = jnp.concatenate([cache_ok, jnp.ones((length,), bool)], axis=0)
    return attend(triple[:, 0], key_rows, value_rows, fresh_pos, key_pos, usable)

def reference(prefill_qkv, decode_qkv, conv_state, cache_len, page_table, page_pool, conv_taps, segment_owner, regroup, residual, norm_gain):

    def one_segment(segment_number):
        device = segment_owner[segment_number].astype(jnp.int32)
        triple = lax.dynamic_slice_in_dim(prefill_qkv, device * SEGMENT, SEGMENT, 0)
        pool_dev = lax.dynamic_slice_in_dim(page_pool, device * POOL_DEV, POOL_DEV, 0)
        request = device * REQ_DEV
        return request_context(triple, conv_state[request], cache_len[request], page_table[request], pool_dev, conv_taps)
    segment_context = lax.map(one_segment, jnp.arange(SEGMENTS, dtype=jnp.int32)).reshape(SEGMENTS * SEGMENT, D)

    def one_device(device):
        pool_dev = lax.dynamic_slice_in_dim(page_pool, device * POOL_DEV, POOL_DEV, 0)
        triples = lax.dynamic_slice_in_dim(decode_qkv, device * DEC_DEV, DEC_DEV, 0)
        conv_tails = lax.dynamic_slice_in_dim(conv_state, device * REQ_DEV + 1, DEC_DEV, 0)
        lengths = lax.dynamic_slice_in_dim(cache_len, device * REQ_DEV + 1, DEC_DEV, 0)
        tables = lax.dynamic_slice_in_dim(page_table, device * REQ_DEV + 1, DEC_DEV, 0)

        def one_decode(triple, conv_tail, cached, table_row):
            return request_context(triple[None], conv_tail, cached, table_row, pool_dev, conv_taps)[0]
        return jax.vmap(one_decode)(triples, conv_tails, lengths, tables)
    decode_context = lax.map(one_device, jnp.arange(N_REQ, dtype=jnp.int32)).reshape(N_REQ * DEC_DEV, D)
    live_context = jnp.concatenate([segment_context, decode_context], axis=0)
    even_context = jnp.zeros((LIVE, D), jnp.bfloat16).at[regroup].set(live_context)
    summed = residual.astype(jnp.float32) + even_context.astype(jnp.float32)
    inverse_rms = lax.rsqrt(lax.optimization_barrier(jnp.mean(summed * summed, axis=1, keepdims=True)) + norm_eps)
    return (summed.astype(jnp.bfloat16), (summed * inverse_rms * norm_gain).astype(jnp.bfloat16))
```

```python
import functools

import jax
import jax.numpy as jnp
from jax import lax
from jax.experimental import pallas as pl
from jax.experimental.pallas import tpu as pltpu
from jax.sharding import PartitionSpec as P

HEADS = 16
HEAD_CHANNELS = 112
WINDOW = 64
PAGE = 128
LANES = 128

norm_eps = 1e-06
masked_score = -1e30
F32 = jnp.float32
BF16 = jnp.bfloat16
I32 = jnp.int32


def iota(shape, dim):
    return lax.broadcasted_iota(I32, shape, dim)


def dot_nt(a, b):
    return lax.dot_general(a, b, (((1,), (1,)), ((), ())), preferred_element_type=F32)


def rotation(regroup_ref, even_rows, devices):
    first = regroup_ref[0:1, 0:1]
    starts = iota((1, devices), 1) * even_rows
    return jnp.sum((starts <= first).astype(I32), axis=1, keepdims=True) - 1


def attention_kernel(
    devices,
    even_rows,
    cache_len_ref,
    page_table_ref,
    q_ref,
    k_ref,
    v_ref,
    tail_ref,
    dq_ref,
    dk_ref,
    dv_ref,
    dt0_ref,
    dt1_ref,
    pool_ref,
    taps_ref,
    regroup_ref,
    out_ref,
    extended,
    keys,
    values,
    context,
    dec_queries,
    dec_scores,
):
    me = lax.axis_index("req")
    rows = q_ref.shape[0]
    width = q_ref.shape[1]
    decodes = dq_ref.shape[0]
    scale = HEAD_CHANNELS ** (-0.5)

    def window_pages(r):
        cached = cache_len_ref[r]
        top = jnp.maximum((cached - 1) >> 7, 0)
        below = jnp.maximum(top - 1, 0)
        return cached, top, page_table_ref[r, top], page_table_ref[r, below]

    def cached_positions(r, shape, dim):
        cached, top, at_top, at_below = window_pages(r)
        offset = iota(shape, dim)
        position = cached - 1 - ((cached - 1 - offset) & (PAGE - 1))
        page = jnp.where(position >= top * PAGE, at_top, at_below)
        return cached, position, page

    _, _, page = cached_positions(0, (PAGE, width), 0)
    first_page = page == 0
    keys[0:PAGE, :] = jnp.where(
        first_page, pool_ref[0, 0].astype(F32), pool_ref[1, 0].astype(F32)
    ).astype(BF16)
    values[0:PAGE, :] = jnp.where(
        first_page, pool_ref[0, 1].astype(F32), pool_ref[1, 1].astype(F32)
    ).astype(BF16)
    extended[6:8, :] = tail_ref[...].astype(F32)
    extended[8 : 8 + rows, :] = k_ref[...].astype(F32)
    keys[PAGE : PAGE + rows, :] = (
        taps_ref[0:1, :] * extended[6 : 6 + rows, :]
        + taps_ref[1:2, :] * extended[7 : 7 + rows, :]
        + taps_ref[2:3, :] * extended[8 : 8 + rows, :]
    ).astype(BF16)
    values[PAGE : PAGE + rows, :] = v_ref[...]

    cached, position, _ = cached_positions(0, (rows, PAGE), 1)
    token = iota((rows, PAGE), 0)
    ok_cached = (position >= 0) & (position >= cached + token - (WINDOW - 1))
    other = iota((rows, rows), 1)
    token = iota((rows, rows), 0)
    ok_fresh = (other <= token) & (other >= token - (WINDOW - 1))
    bias = jnp.concatenate(
        [
            jnp.where(ok_cached, 0.0, masked_score).astype(F32),
            jnp.where(ok_fresh, 0.0, masked_score).astype(F32),
        ],
        axis=1,
    )

    context[...] = jnp.zeros_like(context)
    for head in range(HEADS):
        low, high = head * HEAD_CHANNELS, (head + 1) * HEAD_CHANNELS
        start = low // LANES * LANES
        stop = -(-high // LANES) * LANES
        lane = iota((rows, stop - start), 1) + start
        mine = (lane >= low) & (lane < high)
        query = jnp.where(mine, q_ref[:, start:stop].astype(F32), 0.0).astype(BF16)
        scores = dot_nt(query, keys[:, start:stop]) * scale + bias
        top = jnp.max(scores, axis=1, keepdims=True)
        raised = jnp.exp(scores - top)
        weights = (raised * (1.0 / jnp.sum(raised, axis=1, keepdims=True))).astype(BF16)
        part = jnp.dot(weights, values[:, start:stop], preferred_element_type=F32)
        context[:, start:stop] = jnp.where(mine, part, context[:, start:stop])

    lane = iota((HEADS, width), 1)
    low = iota((HEADS, width), 0) * HEAD_CHANNELS
    mine = (lane >= low) & (lane < low + HEAD_CHANNELS)
    fresh = (
        taps_ref[0:1, :] * dt0_ref[...].astype(F32)
        + taps_ref[1:2, :] * dt1_ref[...].astype(F32)
        + taps_ref[2:3, :] * dk_ref[...].astype(F32)
    ).astype(BF16).astype(F32)
    queries = dq_ref[...].astype(F32)
    new_values = dv_ref[...].astype(F32)
    own = []
    bias_rows = []
    for r in range(decodes):
        spread = jnp.where(mine, queries[r : r + 1, :], 0.0)
        dec_queries[r * HEADS : (r + 1) * HEADS, :] = spread.astype(BF16)
        own.append(jnp.sum(spread * fresh[r : r + 1, :], axis=1, keepdims=True))
        cached, position, page = cached_positions(1 + r, (HEADS, PAGE), 1)
        ok = (position >= 0) & (position >= cached - (WINDOW - 1))
        bias_rows.append(
            jnp.concatenate(
                [
                    jnp.where(ok & (page == n), 0.0, masked_score).astype(F32)
                    for n in range(2)
                ],
                axis=1,
            )
        )
    own = jnp.concatenate(own, axis=0) * scale
    scores = jnp.concatenate(
        [dot_nt(dec_queries[...], pool_ref[n, 0]) for n in range(2)], axis=1
    )
    scores = scores * scale + jnp.concatenate(bias_rows, axis=0)
    top = jnp.maximum(jnp.max(scores, axis=1, keepdims=True), own)
    raised = jnp.exp(scores - top)
    own = jnp.exp(own - top)
    total = 1.0 / (jnp.sum(raised, axis=1, keepdims=True) + own)
    weights = (raised * total).astype(BF16)
    own = (own * total).astype(BF16).astype(F32)
    dec_scores[...] = jnp.dot(
        weights[:, :PAGE], pool_ref[0, 1], preferred_element_type=F32
    ) + jnp.dot(weights[:, PAGE:], pool_ref[1, 1], preferred_element_type=F32)
    dec_rows = []
    for r in range(decodes):
        span = slice(r * HEADS, (r + 1) * HEADS)
        mixed = dec_scores[span, :] + own[span, :] * new_values[r : r + 1, :]
        dec_rows.append(jnp.sum(jnp.where(mine, mixed, 0.0), axis=0, keepdims=True))
    dec_context = jnp.concatenate(dec_rows, axis=0).astype(BF16)

    turn = rotation(regroup_ref, even_rows, devices)
    target = iota((devices, rows), 0)
    chosen = ((target - turn) & (devices - 1)) == iota((devices, rows), 1)
    out_ref[:, :width] = jnp.dot(
        chosen.astype(F32).astype(BF16),
        context[...].astype(BF16),
        preferred_element_type=F32,
    ).astype(BF16)
    target = iota((devices, decodes), 0)
    number = me * decodes + iota((devices, decodes), 1)
    chosen = ((target - turn) & (devices - 1)) == (number & (devices - 1))
    out_ref[:, width:] = jnp.dot(
        chosen.astype(F32).astype(BF16), dec_context, preferred_element_type=F32
    ).astype(BF16)


def finish_kernel(
    devices, arrived_ref, residual_ref, gain_ref, regroup_ref, owner_ref, sum_ref, norm_ref
):
    me = lax.axis_index("req")
    even_rows, width = residual_ref.shape
    decodes = even_rows - devices
    token = (me - rotation(regroup_ref, even_rows, devices)) & (devices - 1)

    column = jnp.sum(
        jnp.where(iota((even_rows, devices), 1) == token, regroup_ref[...], 0),
        axis=1,
        keepdims=True,
    ) - me * even_rows

    def as_row(part):
        size = part.shape[0]
        diagonal = iota((size, devices), 0) == iota((size, devices), 1)
        return jnp.sum(jnp.where(diagonal, part, 0), axis=0, keepdims=True)

    lands = (iota((even_rows, devices), 0) == as_row(column[:devices])).astype(F32)
    diagonal = iota((devices, devices), 0) == iota((devices, devices), 1)
    owner = jnp.sum(jnp.where(diagonal, owner_ref[...], 0), axis=1, keepdims=True)
    came = (iota((devices, devices), 1) == owner).astype(F32)
    pick = jnp.dot(lands.astype(BF16), came.astype(BF16), preferred_element_type=F32)
    gathered = jnp.dot(
        pick.astype(BF16), arrived_ref[:, :width], preferred_element_type=F32
    )

    lane = iota((even_rows, devices), 1)
    lands = (iota((even_rows, devices), 0) == as_row(column[devices:])) & (lane < decodes)
    stride = devices // decodes
    source = (token >> (decodes.bit_length() - 1)) + iota((devices, devices), 0) * stride
    came = (iota((devices, devices), 1) == source).astype(F32)
    pick = jnp.dot(
        lands.astype(F32).astype(BF16), came.astype(BF16), preferred_element_type=F32
    )
    gathered += jnp.dot(
        pick.astype(BF16), arrived_ref[:, width:], preferred_element_type=F32
    )
    summed = residual_ref[...].astype(F32) + gathered
    inverse_rms = lax.rsqrt(jnp.mean(summed * summed, axis=1, keepdims=True) + norm_eps)
    sum_ref[...] = summed.astype(BF16)
    norm_ref[...] = (summed * inverse_rms * gain_ref[...]).astype(BF16)


def body(
    prefill_qkv,
    decode_qkv,
    conv_state,
    cache_len,
    page_table,
    page_pool,
    conv_taps,
    segment_owner,
    regroup,
    residual,
    norm_gain,
):
    devices = lax.axis_size("req")
    rows, _, width = prefill_qkv.shape
    decodes = decode_qkv.shape[0]
    even_rows = residual.shape[0]
    table = regroup.reshape(regroup.shape[0] // devices, devices)
    owner = segment_owner.reshape(1, devices)
    smem = pl.BlockSpec(memory_space=pltpu.SMEM)
    vmem = pl.BlockSpec(memory_space=pltpu.VMEM)
    packed = pl.pallas_call(
        functools.partial(attention_kernel, devices, even_rows),
        out_shape=jax.ShapeDtypeStruct((devices, 2 * width), BF16),
        in_specs=[smem, smem] + [vmem] * 12,
        out_specs=vmem,
        scratch_shapes=[
            pltpu.VMEM((rows + 8, width), F32),
            pltpu.VMEM((PAGE + rows, width), BF16),
            pltpu.VMEM((PAGE + rows, width), BF16),
            pltpu.VMEM((rows, width), F32),
            pltpu.VMEM((decodes * HEADS, width), BF16),
            pltpu.VMEM((decodes * HEADS, width), F32),
        ],
        name="attention",
    )(
        cache_len,
        page_table,
        prefill_qkv[:, 0],
        prefill_qkv[:, 1],
        prefill_qkv[:, 2],
        conv_state[0],
        decode_qkv[:, 0],
        decode_qkv[:, 1],
        decode_qkv[:, 2],
        conv_state[1:, 0],
        conv_state[1:, 1],
        page_pool,
        conv_taps,
        table,
    )
    arrived = lax.all_to_all(packed, "req", split_axis=0, concat_axis=0, tiled=True)
    out = jax.ShapeDtypeStruct((even_rows, width), BF16)
    return pl.pallas_call(
        functools.partial(finish_kernel, devices),
        out_shape=(out, out),
        in_specs=[vmem] * 5,
        out_specs=(vmem, vmem),
        name="finish",
    )(arrived, residual, norm_gain.reshape(1, width), table, owner)


def solution(mesh):
    in_specs = (
        P(("rep", "req"), None, None),
        P(("rep", "req"), None, None),
        P(("rep", "req"), None, None),
        P(("rep", "req")),
        P(("rep", "req"), None),
        P(("rep", "req"), None, None, None),
        P(),
        P("rep"),
        P("rep"),
        P(("rep", "req"), None),
        P(),
    )
    out_specs = (P(("rep", "req"), None), P(("rep", "req"), None))
    return jax.shard_map(body, mesh=mesh, in_specs=in_specs, out_specs=out_specs, check_vma=False)
```

```python
import functools

import jax
import jax.numpy as jnp
from jax import lax
from jax.experimental import pallas as pl
from jax.experimental.pallas import tpu as pltpu
from jax.sharding import PartitionSpec as P

HEADS = 16
HEAD_CHANNELS = 112
WINDOW = 64
PAGE = 128
LANES = 128
STRIDE = 37
MESH = pl.DeviceIdType.MESH

norm_eps = 1e-06
masked_score = -1e30
F32 = jnp.float32
BF16 = jnp.bfloat16
I32 = jnp.int32


def iota(shape, dim):
    return lax.broadcasted_iota(I32, shape, dim)


def dot_nt(a, b):
    return lax.dot_general(a, b, (((1,), (1,)), ((), ())), preferred_element_type=F32)


def rotation(regroup_ref, even_rows, devices):
    first = regroup_ref[0:1, 0:1]
    starts = iota((1, devices), 1) * even_rows
    return jnp.sum((starts <= first).astype(I32), axis=1, keepdims=True) - 1


def exchange_kernel(
    devices,
    even_rows,
    cache_len_ref,
    page_table_ref,
    table_ref,
    qkv_ref,
    dqkv_ref,
    state_ref,
    pool_ref,
    taps_ref,
    arrived_ref,
    extended,
    keys,
    values,
    context,
    dec_queries,
    dec_scores,
    state,
    dec_context,
    wide,
    dec_wide,
    send,
    dec_rows,
    near_send,
    near_recv,
    far_send,
    send_sem,
    recv_sem,
    near_sems,
    far_sems,
    own_sems,
    head,
):
    me = lax.axis_index("req")
    rows = qkv_ref.shape[1]
    width = qkv_ref.shape[2]
    decodes = dqkv_ref.shape[1]
    chunks = width // LANES
    near = devices // decodes
    far = decodes
    place, plane = lax.rem(me, near), lax.div(me, near)
    scale = HEAD_CHANNELS ** (-0.5)
    first = pltpu.make_async_copy(
        table_ref.at[pl.ds(0, 8)], head, own_sems.at[0]
    )
    first.start()

    barrier = pltpu.get_barrier_semaphore()

    @pl.loop(1, devices)
    def _(step):
        peer = lax.rem(me + step, devices)
        pl.semaphore_signal(
            barrier, inc=1, device_id={"req": peer}, device_id_type=MESH
        )

    def cached_positions(r, shape, dim):
        cached = cache_len_ref[r]
        top = jnp.maximum((cached - 1) >> 7, 0)
        below = jnp.maximum(top - 1, 0)
        at_top, at_below = page_table_ref[r, top], page_table_ref[r, below]
        offset = iota(shape, dim)
        position = cached - 1 - ((cached - 1 - offset) & (PAGE - 1))
        page = jnp.where(position >= top * PAGE, at_top, at_below)
        return cached, position, page

    state[...] = state_ref[...].astype(F32)

    lane = iota((HEADS, width), 1)
    low = iota((HEADS, width), 0) * HEAD_CHANNELS
    mine = (lane >= low) & (lane < low + HEAD_CHANNELS)
    fresh = (
        taps_ref[0:1, :] * state[1 : 1 + decodes, 0, :]
        + taps_ref[1:2, :] * state[1 : 1 + decodes, 1, :]
        + taps_ref[2:3, :] * dqkv_ref[1].astype(F32)
    ).astype(BF16).astype(F32)
    queries = dqkv_ref[0].astype(F32)
    new_values = dqkv_ref[2].astype(F32)
    own = []
    bias_rows = []
    for r in range(decodes):
        spread = jnp.where(mine, queries[r : r + 1, :], 0.0)
        dec_queries[r * HEADS : (r + 1) * HEADS, :] = spread.astype(BF16)
        own.append(jnp.sum(spread * fresh[r : r + 1, :], axis=1, keepdims=True))
        cached, position, page = cached_positions(1 + r, (HEADS, PAGE), 1)
        ok = (position >= 0) & (position >= cached - (WINDOW - 1))
        bias_rows.append(
            jnp.concatenate(
                [
                    jnp.where(ok & (page == n), 0.0, masked_score).astype(F32)
                    for n in range(2)
                ],
                axis=1,
            )
        )
    own = jnp.concatenate(own, axis=0) * scale
    scores = jnp.concatenate(
        [dot_nt(dec_queries[...], pool_ref[n, 0]) for n in range(2)], axis=1
    )
    scores = scores * scale + jnp.concatenate(bias_rows, axis=0)
    top = jnp.maximum(jnp.max(scores, axis=1, keepdims=True), own)
    raised = jnp.exp(scores - top)
    own = jnp.exp(own - top)
    total = 1.0 / (jnp.sum(raised, axis=1, keepdims=True) + own)
    weights = (raised * total).astype(BF16)
    own = (own * total).astype(BF16).astype(F32)
    dec_scores[...] = jnp.dot(
        weights[:, :PAGE], pool_ref[0, 1], preferred_element_type=F32
    ) + jnp.dot(weights[:, PAGE:], pool_ref[1, 1], preferred_element_type=F32)
    for r in range(decodes):
        span = slice(r * HEADS, (r + 1) * HEADS)
        mixed = dec_scores[span, :] + own[span, :] * new_values[r : r + 1, :]
        dec_context[r : r + 1, :] = jnp.sum(
            jnp.where(mine, mixed, 0.0), axis=0, keepdims=True
        )
    for c in range(chunks):
        dec_wide[:, c, :] = dec_context[:, c * LANES : (c + 1) * LANES]
    dec_rows[...] = dec_wide[...].astype(BF16)
    first.wait()
    turn = lax.div(head[0, 0], even_rows)
    for p in range(near):
        j = lax.rem(p + 2 * devices - turn - decodes * lax.rem(me, 2), near)
        near_send[p] = dec_rows[jnp.minimum(j, decodes - 1)]

    _, _, page = cached_positions(0, (PAGE, width), 0)
    first_page = page == 0
    keys[0:PAGE, :] = jnp.where(
        first_page, pool_ref[0, 0].astype(F32), pool_ref[1, 0].astype(F32)
    ).astype(BF16)
    values[0:PAGE, :] = jnp.where(
        first_page, pool_ref[0, 1].astype(F32), pool_ref[1, 1].astype(F32)
    ).astype(BF16)
    extended[6:8, :] = state[0]
    extended[8 : 8 + rows, :] = qkv_ref[1].astype(F32)
    keys[PAGE : PAGE + rows, :] = (
        taps_ref[0:1, :] * extended[6 : 6 + rows, :]
        + taps_ref[1:2, :] * extended[7 : 7 + rows, :]
        + taps_ref[2:3, :] * extended[8 : 8 + rows, :]
    ).astype(BF16)
    values[PAGE : PAGE + rows, :] = qkv_ref[2]

    cached, position, _ = cached_positions(0, (rows, PAGE), 1)
    token = iota((rows, PAGE), 0)
    ok_cached = (position >= 0) & (position >= cached + token - (WINDOW - 1))
    other = iota((rows, rows), 1)
    token = iota((rows, rows), 0)
    ok_fresh = (other <= token) & (other >= token - (WINDOW - 1))
    bias = jnp.concatenate(
        [
            jnp.where(ok_cached, 0.0, masked_score).astype(F32),
            jnp.where(ok_fresh, 0.0, masked_score).astype(F32),
        ],
        axis=1,
    )
    context[...] = jnp.zeros_like(context)

    def attend(head):
        low, high = head * HEAD_CHANNELS, (head + 1) * HEAD_CHANNELS
        start = low // LANES * LANES
        stop = -(-high // LANES) * LANES
        lane = iota((rows, stop - start), 1) + start
        mine = (lane >= low) & (lane < high)
        query = jnp.where(mine, qkv_ref[0, :, start:stop].astype(F32), 0.0).astype(BF16)
        scores = dot_nt(query, keys[:, start:stop]) * scale + bias
        top = jnp.max(scores, axis=1, keepdims=True)
        raised = jnp.exp(scores - top)
        weights = (raised * (1.0 / jnp.sum(raised, axis=1, keepdims=True))).astype(BF16)
        part = jnp.dot(weights, values[:, start:stop], preferred_element_type=F32)
        context[:, start:stop] = jnp.where(mine, part, context[:, start:stop])

    for head in range(HEADS // 2):
        attend(head)

    pl.semaphore_wait(barrier, devices - 1)

    near_recv[place] = near_send[place]

    @pl.loop(1, near)
    def _(step):
        goal = lax.rem(place + step, near)
        pltpu.make_async_remote_copy(
            src_ref=near_send.at[goal],
            dst_ref=near_recv.at[place],
            send_sem=near_sems.at[0],
            recv_sem=near_sems.at[1],
            device_id={"req": plane * near + goal},
            device_id_type=MESH,
        ).start()

    for head in range(HEADS // 2, HEADS):
        attend(head)

    def drain(ref, count, sem):
        span = ref.at[pl.ds(0, count)]
        pltpu.make_async_copy(span, span, sem).wait()

    drain(near_recv, near - 1, near_sems.at[1])
    for p in range(far):
        u = lax.rem(p * near + place + devices - turn, devices)
        far_send[p] = near_recv[lax.div(u, decodes)]

    @pl.loop(1, far)
    def _(step):
        goal = lax.rem(plane + step, far)
        pltpu.make_async_remote_copy(
            src_ref=far_send.at[goal],
            dst_ref=arrived_ref.at[devices + plane],
            send_sem=far_sems.at[0],
            recv_sem=far_sems.at[1],
            device_id={"req": goal * near + place},
            device_id_type=MESH,
        ).start()

    order = iota((devices, rows), 0) * STRIDE + me - turn
    chosen = (order & (devices - 1)) == iota((devices, rows), 1)
    context[...] = jnp.dot(
        chosen.astype(F32).astype(BF16),
        context[...].astype(BF16),
        preferred_element_type=F32,
    )
    for c in range(chunks):
        wide[:, c, :] = context[:, c * LANES : (c + 1) * LANES]
    send[...] = wide[...].astype(BF16)

    @pl.loop(1, devices)
    def _(step):
        pltpu.make_async_remote_copy(
            src_ref=send.at[step],
            dst_ref=arrived_ref.at[me],
            send_sem=send_sem,
            recv_sem=recv_sem,
            device_id={"req": lax.rem(me + step * STRIDE, devices)},
            device_id_type=MESH,
        ).start()

    kept = pltpu.make_async_copy(send.at[0], arrived_ref.at[me], own_sems.at[0])
    kept.start()
    kept_far = pltpu.make_async_copy(
        far_send.at[plane], arrived_ref.at[devices + plane], own_sems.at[1]
    )
    kept_far.start()
    kept.wait()
    kept_far.wait()
    drain(near_send, near - 1, near_sems.at[0])
    drain(far_send, far - 1, far_sems.at[0])
    drain(arrived_ref, far - 1, far_sems.at[1])
    drain(send, devices - 1, send_sem)
    drain(arrived_ref, devices - 1, recv_sem)


def finish_kernel(
    devices,
    arrived_ref,
    residual_ref,
    gain_ref,
    regroup_ref,
    owner_ref,
    sum_ref,
    norm_ref,
    wide,
    rows,
):
    me = lax.axis_index("req")
    even_rows, width = residual_ref.shape
    decodes = even_rows - devices
    token = (me - rotation(regroup_ref, even_rows, devices)) & (devices - 1)

    column = jnp.sum(
        jnp.where(iota((even_rows, devices), 1) == token, regroup_ref[...], 0),
        axis=1,
        keepdims=True,
    ) - me * even_rows

    def lands(part):
        size = part.shape[0]
        diagonal = iota((size, size), 0) == iota((size, size), 1)
        row = jnp.sum(jnp.where(diagonal, part, 0), axis=0, keepdims=True)
        return (iota((even_rows, size), 0) == row).astype(F32).astype(BF16)

    diagonal = iota((devices, devices), 0) == iota((devices, devices), 1)
    owner = jnp.sum(jnp.where(diagonal, owner_ref[...], 0), axis=1, keepdims=True)
    came = (iota((devices, devices), 1) == owner).astype(F32).astype(BF16)
    pick = jnp.dot(lands(column[:devices]), came, preferred_element_type=F32).astype(BF16)
    wide[...] = arrived_ref[...].astype(F32)
    for c in range(width // LANES):
        rows[:, c * LANES : (c + 1) * LANES] = wide[:, c, :].astype(BF16)
    gathered = jnp.dot(pick, rows[:devices, :], preferred_element_type=F32)
    gathered += jnp.dot(
        lands(column[devices:]), rows[devices:, :], preferred_element_type=F32
    )
    summed = residual_ref[...].astype(F32) + gathered
    inverse_rms = lax.rsqrt(jnp.mean(summed * summed, axis=1, keepdims=True) + norm_eps)
    sum_ref[...] = summed.astype(BF16)
    norm_ref[...] = (summed * inverse_rms * gain_ref[...]).astype(BF16)


def body(
    prefill_qkv,
    decode_qkv,
    conv_state,
    cache_len,
    page_table,
    page_pool,
    conv_taps,
    segment_owner,
    regroup,
    residual,
    norm_gain,
):
    devices = lax.axis_size("req")
    rows, _, width = prefill_qkv.shape
    decodes = decode_qkv.shape[0]
    even_rows = residual.shape[0]
    chunks = width // LANES
    near = devices // decodes
    table = regroup.reshape(regroup.shape[0] // devices, devices)
    owner = segment_owner.reshape(1, devices)
    smem = pl.BlockSpec(memory_space=pltpu.SMEM)
    vmem = pl.BlockSpec(memory_space=pltpu.VMEM)
    hbm = pl.BlockSpec(memory_space=pl.ANY)
    arrived = pl.pallas_call(
        functools.partial(exchange_kernel, devices, even_rows),
        out_shape=jax.ShapeDtypeStruct((even_rows, chunks, LANES), BF16),
        in_specs=[smem, smem, hbm] + [vmem] * 5,
        out_specs=hbm,
        scratch_shapes=[
            pltpu.VMEM((rows + 8, width), F32),
            pltpu.VMEM((PAGE + rows, width), BF16),
            pltpu.VMEM((PAGE + rows, width), BF16),
            pltpu.VMEM((rows, width), F32),
            pltpu.VMEM((decodes * HEADS, width), BF16),
            pltpu.VMEM((decodes * HEADS, width), F32),
            pltpu.VMEM(conv_state.shape, F32),
            pltpu.VMEM((decodes, width), F32),
            pltpu.VMEM((devices, chunks, LANES), F32),
            pltpu.VMEM((decodes, chunks, LANES), F32),
            pltpu.VMEM((devices, chunks, LANES), BF16),
            pltpu.VMEM((decodes, chunks, LANES), BF16),
            pltpu.VMEM((near, chunks, LANES), BF16),
            pltpu.VMEM((near, chunks, LANES), BF16),
            pltpu.VMEM((decodes, chunks, LANES), BF16),
            pltpu.SemaphoreType.DMA,
            pltpu.SemaphoreType.DMA,
            pltpu.SemaphoreType.DMA((2,)),
            pltpu.SemaphoreType.DMA((2,)),
            pltpu.SemaphoreType.DMA((2,)),
            pltpu.SMEM((8, devices), I32),
        ],
        compiler_params=pltpu.CompilerParams(collective_id=0, has_side_effects=True),
        name="exchange",
    )(
        cache_len,
        page_table,
        table,
        prefill_qkv.transpose(1, 0, 2),
        decode_qkv.transpose(1, 0, 2),
        conv_state,
        page_pool,
        conv_taps,
    )
    out = jax.ShapeDtypeStruct((even_rows, width), BF16)
    return pl.pallas_call(
        functools.partial(finish_kernel, devices),
        out_shape=(out, out),
        in_specs=[vmem] * 5,
        out_specs=(vmem, vmem),
        scratch_shapes=[
            pltpu.VMEM((even_rows, chunks, LANES), F32),
            pltpu.VMEM((even_rows, width), BF16),
        ],
        name="finish",
    )(arrived, residual, norm_gain.reshape(1, width), table, owner)


def solution(mesh):
    in_specs = (
        P(("rep", "req"), None, None),
        P(("rep", "req"), None, None),
        P(("rep", "req"), None, None),
        P(("rep", "req")),
        P(("rep", "req"), None),
        P(("rep", "req"), None, None, None),
        P(),
        P("rep"),
        P("rep"),
        P(("rep", "req"), None),
        P(),
    )
    out_specs = (P(("rep", "req"), None), P(("rep", "req"), None))
    return jax.shard_map(body, mesh=mesh, in_specs=in_specs, out_specs=out_specs, check_vma=False)
```

```python
import functools

import jax
import jax.numpy as jnp
from jax import lax
from jax.experimental import pallas as pl
from jax.experimental.pallas import tpu as pltpu
from jax.sharding import PartitionSpec as P

HEADS = 16
HEAD_CHANNELS = 112
WINDOW = 64
PAGE = 128
LANES = 128
MESH = pl.DeviceIdType.MESH

norm_eps = 1e-06
masked_score = -1e30
F32 = jnp.float32
BF16 = jnp.bfloat16
I32 = jnp.int32


def iota(shape, dim):
    return lax.broadcasted_iota(I32, shape, dim)


def dot_nt(a, b):
    return lax.dot_general(a, b, (((1,), (1,)), ((), ())), preferred_element_type=F32)


def rotation(regroup_ref, even_rows, devices):
    first = regroup_ref[0:1, 0:1]
    starts = iota((1, devices), 1) * even_rows
    return jnp.sum((starts <= first).astype(I32), axis=1, keepdims=True) - 1


def offset_of(rank):
    return 4 + ((rank + 1) // 2) * (1 - 2 * (rank % 2))


def exchange_kernel(
    devices,
    even_rows,
    cache_len_ref,
    page_table_ref,
    table_ref,
    qkv_ref,
    dqkv_ref,
    state_ref,
    pool_ref,
    taps_ref,
    arrived_ref,
    far_ref,
    extended,
    keys,
    values,
    context,
    dec_queries,
    dec_scores,
    state,
    dec_context,
    wide,
    dec_wide,
    send,
    dec_rows,
    near_send,
    near_recv,
    far_send,
    send_sems,
    recv_sems,
    near_sems,
    far_sems,
    own_sems,
    head,
):
    me = lax.axis_index("req")
    rows = qkv_ref.shape[1]
    width = qkv_ref.shape[2]
    decodes = dqkv_ref.shape[1]
    chunks = width // LANES
    near = devices // decodes
    far = decodes
    place, plane = lax.rem(me, near), lax.div(me, near)
    column, core = lax.div(place, 2), lax.rem(place, 2)
    half = width // 2
    scale = HEAD_CHANNELS ** (-0.5)
    first = pltpu.make_async_copy(
        table_ref.at[pl.ds(0, 8)], head, own_sems.at[0]
    )
    first.start()

    barrier = pltpu.get_barrier_semaphore()

    @pl.loop(1, devices)
    def _(step):
        peer = lax.rem(me + step, devices)
        pl.semaphore_signal(
            barrier, inc=1, device_id={"req": peer}, device_id_type=MESH
        )

    def cached_positions(r, shape, dim):
        cached = cache_len_ref[r]
        top = jnp.maximum((cached - 1) >> 7, 0)
        below = jnp.maximum(top - 1, 0)
        at_top, at_below = page_table_ref[r, top], page_table_ref[r, below]
        offset = iota(shape, dim)
        position = cached - 1 - ((cached - 1 - offset) & (PAGE - 1))
        page = jnp.where(position >= top * PAGE, at_top, at_below)
        return cached, position, page

    state[...] = state_ref[...].astype(F32)

    first.wait()
    turn = lax.div(head[0, 0], even_rows)
    _, _, page = cached_positions(0, (PAGE, width), 0)
    first_page = page == 0
    keys[0:PAGE, :] = jnp.where(
        first_page, pool_ref[0, 0].astype(F32), pool_ref[1, 0].astype(F32)
    ).astype(BF16)
    values[0:PAGE, :] = jnp.where(
        first_page, pool_ref[0, 1].astype(F32), pool_ref[1, 1].astype(F32)
    ).astype(BF16)
    extended[6:8, :] = state[0]
    extended[8 : 8 + rows, :] = qkv_ref[1].astype(F32)
    keys[PAGE : PAGE + rows, :] = (
        taps_ref[0:1, :] * extended[6 : 6 + rows, :]
        + taps_ref[1:2, :] * extended[7 : 7 + rows, :]
        + taps_ref[2:3, :] * extended[8 : 8 + rows, :]
    ).astype(BF16)
    values[PAGE : PAGE + rows, :] = qkv_ref[2]

    def fresh_bias(begin, count):
        other = iota((WINDOW, count), 1)
        token = iota((WINDOW, count), 0) + begin
        ok = (other <= token) & (other >= token - (WINDOW - 1))
        return jnp.where(ok, 0.0, masked_score).astype(F32)

    cached, position, _ = cached_positions(0, (WINDOW, PAGE), 1)
    token = iota((WINDOW, PAGE), 0)
    ok = (position >= 0) & (position >= cached + token - (WINDOW - 1))
    bands = [
        (
            0,
            0,
            PAGE + WINDOW,
            jnp.concatenate(
                [jnp.where(ok, 0.0, masked_score).astype(F32), fresh_bias(0, WINDOW)],
                axis=1,
            ),
        )
    ]
    for begin in range(WINDOW, rows, WINDOW):
        first_key = begin - WINDOW
        bands.append((begin, PAGE + first_key, 2 * WINDOW, fresh_bias(WINDOW, 2 * WINDOW)))
    context[...] = jnp.zeros_like(context)

    def attend(head):
        low, high = head * HEAD_CHANNELS, (head + 1) * HEAD_CHANNELS
        start = low // LANES * LANES
        stop = -(-high // LANES) * LANES
        lane = iota((WINDOW, stop - start), 1) + start
        mine = (lane >= low) & (lane < high)
        for begin, key, count, bias in bands:
            block = slice(begin, begin + WINDOW)
            query = qkv_ref[0, block, start:stop].astype(F32)
            query = jnp.where(mine, query, 0.0).astype(BF16)
            scores = dot_nt(query, keys[key : key + count, start:stop]) * scale + bias
            top = jnp.max(scores, axis=1, keepdims=True)
            raised = jnp.exp(scores - top)
            share = 1.0 / jnp.sum(raised, axis=1, keepdims=True)
            part = jnp.dot(
                (raised * share).astype(BF16),
                values[key : key + count, start:stop],
                preferred_element_type=F32,
            )
            context[block, start:stop] = jnp.where(mine, part, context[block, start:stop])

    slot = iota((devices, rows), 0)

    def offsets(rank):
        return 4 + ((rank + 1) >> 1) * (1 - 2 * (rank & 1))

    target = (
        ((plane + offsets(slot >> 4)) & (far - 1)) * near
        + ((column + offsets((slot >> 1) & 7)) & 7) * 2
        + ((core + 1 + slot) & 1)
    )
    chosen = ((target - turn) & (devices - 1)) == iota((devices, rows), 1)
    chosen = chosen.astype(F32).astype(BF16)

    def send_half(side):
        span = slice(side * half, (side + 1) * half)
        context[:, span] = jnp.dot(
            chosen, context[:, span].astype(BF16), preferred_element_type=F32
        )
        for c in range(chunks // 2):
            low = side * half + c * LANES
            wide[:, c, :] = context[:, low : low + LANES]
        send[side] = wide[...].astype(BF16)

        def to_chip(rank_z, rank_y, cores):
            goal_z = lax.rem(plane + offset_of(rank_z), far)
            goal_y = lax.rem(column + offset_of(rank_y), 8)
            for c in range(cores):
                goal_core = lax.rem(core + 1 + c, 2)
                pltpu.make_async_remote_copy(
                    src_ref=send.at[side, (rank_z * 8 + rank_y) * 2 + c],
                    dst_ref=arrived_ref.at[side, me],
                    send_sem=send_sems.at[side],
                    recv_sem=recv_sems.at[side],
                    device_id={"req": goal_z * near + goal_y * 2 + goal_core},
                    device_id_type=MESH,
                ).start()

        for shell in range(far):
            if shell:

                @pl.loop(0, shell)
                def _(rank):
                    to_chip(shell, rank, 2)
                    to_chip(rank, shell, 2)

            to_chip(shell, shell, 2 if shell < far - 1 else 1)

    for head in range(HEADS // 2):
        attend(head)

    pl.semaphore_wait(barrier, devices - 1)
    send_half(0)

    lane = iota((HEADS, width), 1)
    low = iota((HEADS, width), 0) * HEAD_CHANNELS
    mine = (lane >= low) & (lane < low + HEAD_CHANNELS)
    fresh = (
        taps_ref[0:1, :] * state[1 : 1 + decodes, 0, :]
        + taps_ref[1:2, :] * state[1 : 1 + decodes, 1, :]
        + taps_ref[2:3, :] * dqkv_ref[1].astype(F32)
    ).astype(BF16).astype(F32)
    queries = dqkv_ref[0].astype(F32)
    new_values = dqkv_ref[2].astype(F32)
    own = []
    bias_rows = []
    for r in range(decodes):
        spread = jnp.where(mine, queries[r : r + 1, :], 0.0)
        dec_queries[r * HEADS : (r + 1) * HEADS, :] = spread.astype(BF16)
        own.append(jnp.sum(spread * fresh[r : r + 1, :], axis=1, keepdims=True))
        cached, position, page = cached_positions(1 + r, (HEADS, PAGE), 1)
        ok = (position >= 0) & (position >= cached - (WINDOW - 1))
        bias_rows.append(
            jnp.concatenate(
                [
                    jnp.where(ok & (page == n), 0.0, masked_score).astype(F32)
                    for n in range(2)
                ],
                axis=1,
            )
        )
    own = jnp.concatenate(own, axis=0) * scale
    scores = jnp.concatenate(
        [dot_nt(dec_queries[...], pool_ref[n, 0]) for n in range(2)], axis=1
    )
    scores = scores * scale + jnp.concatenate(bias_rows, axis=0)
    top = jnp.maximum(jnp.max(scores, axis=1, keepdims=True), own)
    raised = jnp.exp(scores - top)
    own = jnp.exp(own - top)
    total = 1.0 / (jnp.sum(raised, axis=1, keepdims=True) + own)
    weights = (raised * total).astype(BF16)
    own = (own * total).astype(BF16).astype(F32)
    dec_scores[...] = jnp.dot(
        weights[:, :PAGE], pool_ref[0, 1], preferred_element_type=F32
    ) + jnp.dot(weights[:, PAGE:], pool_ref[1, 1], preferred_element_type=F32)
    for r in range(decodes):
        span = slice(r * HEADS, (r + 1) * HEADS)
        mixed = dec_scores[span, :] + own[span, :] * new_values[r : r + 1, :]
        dec_context[r : r + 1, :] = jnp.sum(
            jnp.where(mine, mixed, 0.0), axis=0, keepdims=True
        )
    for c in range(chunks):
        dec_wide[:, c, :] = dec_context[:, c * LANES : (c + 1) * LANES]
    dec_rows[...] = dec_wide[...].astype(BF16)
    for p in range(near):
        j = lax.rem(p + 2 * devices - turn - decodes * lax.rem(me, 2), near)
        near_send[p] = dec_rows[jnp.minimum(j, decodes - 1)]

    near_recv[place] = near_send[place]

    @pl.loop(1, near)
    def _(step):
        goal = lax.rem(place + step, near)
        pltpu.make_async_remote_copy(
            src_ref=near_send.at[goal],
            dst_ref=near_recv.at[place],
            send_sem=near_sems.at[0],
            recv_sem=near_sems.at[1],
            device_id={"req": plane * near + goal},
            device_id_type=MESH,
        ).start()

    for head in range(HEADS // 2, HEADS):
        attend(head)
    send_half(1)

    def drain(ref, count, sem):
        span = ref.at[pl.ds(0, count)]
        pltpu.make_async_copy(span, span, sem).wait()

    drain(near_recv, near - 1, near_sems.at[1])
    for p in range(far):
        u = lax.rem(p * near + place + devices - turn, devices)
        far_send[p] = near_recv[lax.div(u, decodes)]

    @pl.loop(1, far)
    def _(step):
        goal = lax.rem(plane + step, far)
        pltpu.make_async_remote_copy(
            src_ref=far_send.at[goal],
            dst_ref=far_ref.at[plane],
            send_sem=far_sems.at[0],
            recv_sem=far_sems.at[1],
            device_id={"req": goal * near + place},
            device_id_type=MESH,
        ).start()

    kept = [
        pltpu.make_async_copy(
            send.at[side, devices - 1], arrived_ref.at[side, me], own_sems.at[side]
        )
        for side in range(2)
    ]
    kept.append(
        pltpu.make_async_copy(far_send.at[plane], far_ref.at[plane], own_sems.at[2])
    )
    for copy in kept:
        copy.start()
    for copy in kept:
        copy.wait()
    drain(near_send, near - 1, near_sems.at[0])
    drain(far_send, far - 1, far_sems.at[0])
    drain(far_ref, far - 1, far_sems.at[1])
    for side in range(2):
        drain(send.at[side], devices - 1, send_sems.at[side])
        drain(arrived_ref.at[side], devices - 1, recv_sems.at[side])


def finish_kernel(
    devices,
    arrived_ref,
    far_ref,
    residual_ref,
    gain_ref,
    regroup_ref,
    owner_ref,
    sum_ref,
    norm_ref,
    wide,
    far_wide,
    rows,
):
    me = lax.axis_index("req")
    even_rows, width = residual_ref.shape
    decodes = even_rows - devices
    token = (me - rotation(regroup_ref, even_rows, devices)) & (devices - 1)

    column = jnp.sum(
        jnp.where(iota((even_rows, devices), 1) == token, regroup_ref[...], 0),
        axis=1,
        keepdims=True,
    ) - me * even_rows

    def lands(part):
        size = part.shape[0]
        diagonal = iota((size, size), 0) == iota((size, size), 1)
        row = jnp.sum(jnp.where(diagonal, part, 0), axis=0, keepdims=True)
        return (iota((even_rows, size), 0) == row).astype(F32).astype(BF16)

    diagonal = iota((devices, devices), 0) == iota((devices, devices), 1)
    owner = jnp.sum(jnp.where(diagonal, owner_ref[...], 0), axis=1, keepdims=True)
    came = (iota((devices, devices), 1) == owner).astype(F32).astype(BF16)
    pick = jnp.dot(lands(column[:devices]), came, preferred_element_type=F32).astype(BF16)
    wide[...] = arrived_ref[...].astype(F32)
    far_wide[...] = far_ref[...].astype(F32)
    half = wide.shape[2]
    for c in range(width // LANES):
        span = slice(c * LANES, (c + 1) * LANES)
        rows[:devices, span] = wide[c // half, :, c % half, :].astype(BF16)
        rows[devices:, span] = far_wide[:, c, :].astype(BF16)
    gathered = jnp.dot(pick, rows[:devices, :], preferred_element_type=F32)
    gathered += jnp.dot(
        lands(column[devices:]), rows[devices:, :], preferred_element_type=F32
    )
    summed = residual_ref[...].astype(F32) + gathered
    inverse_rms = lax.rsqrt(jnp.mean(summed * summed, axis=1, keepdims=True) + norm_eps)
    sum_ref[...] = summed.astype(BF16)
    norm_ref[...] = (summed * inverse_rms * gain_ref[...].reshape(1, width)).astype(BF16)


def body(
    prefill_qkv,
    decode_qkv,
    conv_state,
    cache_len,
    page_table,
    page_pool,
    conv_taps,
    segment_owner,
    regroup,
    residual,
    norm_gain,
):
    devices = lax.axis_size("req")
    rows, _, width = prefill_qkv.shape
    decodes = decode_qkv.shape[0]
    even_rows = residual.shape[0]
    chunks = width // LANES
    near = devices // decodes
    table = regroup.reshape(regroup.shape[0] // devices, devices)
    owner = segment_owner.reshape(1, devices)
    smem = pl.BlockSpec(memory_space=pltpu.SMEM)
    vmem = pl.BlockSpec(memory_space=pltpu.VMEM)
    hbm = pl.BlockSpec(memory_space=pl.ANY)
    arrived, far = pl.pallas_call(
        functools.partial(exchange_kernel, devices, even_rows),
        out_shape=(
            jax.ShapeDtypeStruct((2, devices, chunks // 2, LANES), BF16),
            jax.ShapeDtypeStruct((decodes, chunks, LANES), BF16),
        ),
        in_specs=[smem, smem, hbm] + [vmem] * 5,
        out_specs=(hbm, hbm),
        scratch_shapes=[
            pltpu.VMEM((rows + 8, width), F32),
            pltpu.VMEM((PAGE + rows, width), BF16),
            pltpu.VMEM((PAGE + rows, width), BF16),
            pltpu.VMEM((rows, width), F32),
            pltpu.VMEM((decodes * HEADS, width), BF16),
            pltpu.VMEM((decodes * HEADS, width), F32),
            pltpu.VMEM(conv_state.shape, F32),
            pltpu.VMEM((decodes, width), F32),
            pltpu.VMEM((devices, chunks // 2, LANES), F32),
            pltpu.VMEM((decodes, chunks, LANES), F32),
            pltpu.VMEM((2, devices, chunks // 2, LANES), BF16),
            pltpu.VMEM((decodes, chunks, LANES), BF16),
            pltpu.VMEM((near, chunks, LANES), BF16),
            pltpu.VMEM((near, chunks, LANES), BF16),
            pltpu.VMEM((decodes, chunks, LANES), BF16),
            pltpu.SemaphoreType.DMA((2,)),
            pltpu.SemaphoreType.DMA((2,)),
            pltpu.SemaphoreType.DMA((2,)),
            pltpu.SemaphoreType.DMA((2,)),
            pltpu.SemaphoreType.DMA((3,)),
            pltpu.SMEM((8, devices), I32),
        ],
        compiler_params=pltpu.CompilerParams(collective_id=0, has_side_effects=True),
        name="exchange",
    )(
        cache_len,
        page_table,
        table,
        prefill_qkv.transpose(1, 0, 2),
        decode_qkv.transpose(1, 0, 2),
        conv_state,
        page_pool,
        conv_taps,
    )
    out = jax.ShapeDtypeStruct((even_rows, width), BF16)
    return pl.pallas_call(
        functools.partial(finish_kernel, devices),
        out_shape=(out, out),
        in_specs=[vmem] * 6,
        out_specs=(vmem, vmem),
        scratch_shapes=[
            pltpu.VMEM((2, devices, chunks // 2, LANES), F32),
            pltpu.VMEM((decodes, chunks, LANES), F32),
            pltpu.VMEM((even_rows, width), BF16),
        ],
        name="finish",
    )(arrived, far, residual, norm_gain, table, owner)


def solution(mesh):
    in_specs = (
        P(("rep", "req"), None, None),
        P(("rep", "req"), None, None),
        P(("rep", "req"), None, None),
        P(("rep", "req")),
        P(("rep", "req"), None),
        P(("rep", "req"), None, None, None),
        P(),
        P("rep"),
        P("rep"),
        P(("rep", "req"), None),
        P(),
    )
    out_specs = (P(("rep", "req"), None), P(("rep", "req"), None))
    return jax.shard_map(body, mesh=mesh, in_specs=in_specs, out_specs=out_specs, check_vma=False)
```

```python
import functools

import jax
import jax.numpy as jnp
from jax import lax
from jax.experimental import pallas as pl
from jax.experimental.pallas import tpu as pltpu
from jax.sharding import PartitionSpec as P

HEADS = 16
HEAD_CHANNELS = 112
WINDOW = 64
PAGE = 128
LANES = 128
EARLY_LANES = 1024
EARLY_HEADS = -(-EARLY_LANES // HEAD_CHANNELS)
MESH = pl.DeviceIdType.MESH

norm_eps = 1e-06
masked_score = -1e30
F32 = jnp.float32
BF16 = jnp.bfloat16
I32 = jnp.int32


def iota(shape, dim):
    return lax.broadcasted_iota(I32, shape, dim)


def dot_nt(a, b):
    return lax.dot_general(a, b, (((1,), (1,)), ((), ())), preferred_element_type=F32)


def offset_of(rank):
    return 4 + ((rank + 1) // 2) * (1 - 2 * (rank % 2))


def exchange_kernel(
    devices,
    even_rows,
    cache_len_ref,
    page_table_ref,
    table_ref,
    qkv_ref,
    dqkv_ref,
    state_ref,
    pool_ref,
    taps_ref,
    regroup_ref,
    owner_ref,
    gathered_ref,
    extended,
    keys,
    values,
    context,
    dec_queries,
    dec_scores,
    state,
    dec_context,
    wide,
    dec_wide,
    send_0,
    send_1,
    recv_0,
    recv_1,
    far_recv,
    dec_rows,
    near_send,
    near_recv,
    far_send,
    send_sems,
    recv_sems,
    near_sems,
    far_sems,
    own_sems,
    head,
):
    me = lax.axis_index("req")
    rows = qkv_ref.shape[1]
    width = qkv_ref.shape[2]
    decodes = dqkv_ref.shape[1]
    chunks = width // LANES
    near = devices // decodes
    far = decodes
    place, plane = lax.rem(me, near), lax.div(me, near)
    column, core = lax.div(place, 2), lax.rem(place, 2)
    spans = [slice(0, EARLY_LANES), slice(EARLY_LANES, width)]
    scale = HEAD_CHANNELS ** (-0.5)
    first = pltpu.make_async_copy(
        table_ref.at[pl.ds(0, 8)], head, own_sems.at[0]
    )
    first.start()

    send, recv = (send_0, send_1), (recv_0, recv_1)
    barrier = pltpu.get_barrier_semaphore()

    @pl.loop(1, devices)
    def _(step):
        peer = lax.rem(me + step, devices)
        pl.semaphore_signal(
            barrier, inc=1, device_id={"req": peer}, device_id_type=MESH
        )

    def cached_positions(r, shape, dim):
        cached = cache_len_ref[r]
        top = jnp.maximum((cached - 1) >> 7, 0)
        below = jnp.maximum(top - 1, 0)
        at_top, at_below = page_table_ref[r, top], page_table_ref[r, below]
        offset = iota(shape, dim)
        position = cached - 1 - ((cached - 1 - offset) & (PAGE - 1))
        page = jnp.where(position >= top * PAGE, at_top, at_below)
        return cached, position, page

    state[...] = state_ref[...].astype(F32)

    first.wait()
    turn = lax.div(head[0, 0], even_rows)
    lane = iota((HEADS, width), 1)
    low = iota((HEADS, width), 0) * HEAD_CHANNELS
    mine = (lane >= low) & (lane < low + HEAD_CHANNELS)
    fresh = (
        taps_ref[0:1, :] * state[1 : 1 + decodes, 0, :]
        + taps_ref[1:2, :] * state[1 : 1 + decodes, 1, :]
        + taps_ref[2:3, :] * dqkv_ref[1].astype(F32)
    ).astype(BF16).astype(F32)
    queries = dqkv_ref[0].astype(F32)
    new_values = dqkv_ref[2].astype(F32)
    own = []
    bias_rows = []
    for r in range(decodes):
        spread = jnp.where(mine, queries[r : r + 1, :], 0.0)
        dec_queries[r * HEADS : (r + 1) * HEADS, :] = spread.astype(BF16)
        own.append(jnp.sum(spread * fresh[r : r + 1, :], axis=1, keepdims=True))
        cached, position, page = cached_positions(1 + r, (HEADS, PAGE), 1)
        ok = (position >= 0) & (position >= cached - (WINDOW - 1))
        bias_rows.append(
            jnp.concatenate(
                [
                    jnp.where(ok & (page == n), 0.0, masked_score).astype(F32)
                    for n in range(2)
                ],
                axis=1,
            )
        )
    own = jnp.concatenate(own, axis=0) * scale
    scores = jnp.concatenate(
        [dot_nt(dec_queries[...], pool_ref[n, 0]) for n in range(2)], axis=1
    )
    scores = scores * scale + jnp.concatenate(bias_rows, axis=0)
    top = jnp.maximum(jnp.max(scores, axis=1, keepdims=True), own)
    raised = jnp.exp(scores - top)
    own = jnp.exp(own - top)
    total = 1.0 / (jnp.sum(raised, axis=1, keepdims=True) + own)
    weights = (raised * total).astype(BF16)
    own = (own * total).astype(BF16).astype(F32)
    dec_scores[...] = jnp.dot(
        weights[:, :PAGE], pool_ref[0, 1], preferred_element_type=F32
    ) + jnp.dot(weights[:, PAGE:], pool_ref[1, 1], preferred_element_type=F32)
    for r in range(decodes):
        span = slice(r * HEADS, (r + 1) * HEADS)
        mixed = dec_scores[span, :] + own[span, :] * new_values[r : r + 1, :]
        dec_context[r : r + 1, :] = jnp.sum(
            jnp.where(mine, mixed, 0.0), axis=0, keepdims=True
        )
    for c in range(chunks):
        dec_wide[:, c, :] = dec_context[:, c * LANES : (c + 1) * LANES]
    dec_rows[...] = dec_wide[...].astype(BF16)
    for p in range(near):
        j = lax.rem(p + 2 * devices - turn - decodes * lax.rem(me, 2), near)
        near_send[p] = dec_rows[jnp.minimum(j, decodes - 1)]

    _, _, page = cached_positions(0, (PAGE, width), 0)
    first_page = page == 0
    keys[0:PAGE, :] = jnp.where(
        first_page, pool_ref[0, 0].astype(F32), pool_ref[1, 0].astype(F32)
    ).astype(BF16)
    values[0:PAGE, :] = jnp.where(
        first_page, pool_ref[0, 1].astype(F32), pool_ref[1, 1].astype(F32)
    ).astype(BF16)
    extended[6:8, :] = state[0]
    extended[8 : 8 + rows, :] = qkv_ref[1].astype(F32)
    keys[PAGE : PAGE + rows, :] = (
        taps_ref[0:1, :] * extended[6 : 6 + rows, :]
        + taps_ref[1:2, :] * extended[7 : 7 + rows, :]
        + taps_ref[2:3, :] * extended[8 : 8 + rows, :]
    ).astype(BF16)
    values[PAGE : PAGE + rows, :] = qkv_ref[2]

    def fresh_bias(begin, count):
        other = iota((WINDOW, count), 1)
        token = iota((WINDOW, count), 0) + begin
        ok = (other <= token) & (other >= token - (WINDOW - 1))
        return jnp.where(ok, 0.0, masked_score).astype(F32)

    cached, position, _ = cached_positions(0, (WINDOW, PAGE), 1)
    token = iota((WINDOW, PAGE), 0)
    ok = (position >= 0) & (position >= cached + token - (WINDOW - 1))
    bands = [
        (
            0,
            0,
            PAGE + WINDOW,
            jnp.concatenate(
                [jnp.where(ok, 0.0, masked_score).astype(F32), fresh_bias(0, WINDOW)],
                axis=1,
            ),
        )
    ]
    for begin in range(WINDOW, rows, WINDOW):
        first_key = begin - WINDOW
        bands.append((begin, PAGE + first_key, 2 * WINDOW, fresh_bias(WINDOW, 2 * WINDOW)))
    context[...] = jnp.zeros_like(context)

    def attend(head):
        low, high = head * HEAD_CHANNELS, (head + 1) * HEAD_CHANNELS
        start = low // LANES * LANES
        stop = -(-high // LANES) * LANES
        lane = iota((WINDOW, stop - start), 1) + start
        mine = (lane >= low) & (lane < high)
        for begin, key, count, bias in bands:
            block = slice(begin, begin + WINDOW)
            query = qkv_ref[0, block, start:stop].astype(F32)
            query = jnp.where(mine, query, 0.0).astype(BF16)
            scores = dot_nt(query, keys[key : key + count, start:stop]) * scale + bias
            top = jnp.max(scores, axis=1, keepdims=True)
            raised = jnp.exp(scores - top)
            share = 1.0 / jnp.sum(raised, axis=1, keepdims=True)
            part = jnp.dot(
                (raised * share).astype(BF16),
                values[key : key + count, start:stop],
                preferred_element_type=F32,
            )
            context[block, start:stop] = jnp.where(mine, part, context[block, start:stop])

    slot = iota((devices, rows), 0)

    def offsets(rank):
        return 4 + ((rank + 1) >> 1) * (1 - 2 * (rank & 1))

    target = (
        ((plane + offsets(slot >> 4)) & (far - 1)) * near
        + ((column + offsets((slot >> 1) & 7)) & 7) * 2
        + ((core + 1 + slot) & 1)
    )
    chosen = ((target - turn) & (devices - 1)) == iota((devices, rows), 1)
    chosen = chosen.astype(F32).astype(BF16)

    def send_half(side):
        span = spans[side]
        sent = jnp.dot(
            chosen, context[:, span].astype(BF16), preferred_element_type=F32
        )
        count = (span.stop - span.start) // LANES
        for c in range(count):
            wide[:, c, :] = sent[:, c * LANES : (c + 1) * LANES]
        send[side][...] = wide[:, :count, :].astype(BF16)

        def to_chip(rank_z, rank_y, cores):
            goal_z = lax.rem(plane + offset_of(rank_z), far)
            goal_y = lax.rem(column + offset_of(rank_y), 8)
            for c in range(cores):
                goal_core = lax.rem(core + 1 + c, 2)
                pltpu.make_async_remote_copy(
                    src_ref=send[side].at[(rank_z * 8 + rank_y) * 2 + c],
                    dst_ref=recv[side].at[me],
                    send_sem=send_sems.at[side],
                    recv_sem=recv_sems.at[side],
                    device_id={"req": goal_z * near + goal_y * 2 + goal_core},
                    device_id_type=MESH,
                ).start()

        for shell in range(far):
            if shell:

                @pl.loop(0, shell)
                def _(rank):
                    to_chip(shell, rank, 2)
                    to_chip(rank, shell, 2)

            to_chip(shell, shell, 2 if shell < far - 1 else 1)

    for head in range(EARLY_HEADS):
        attend(head)

    pl.semaphore_wait(barrier, devices - 1)

    near_recv[place] = near_send[place]

    @pl.loop(1, near)
    def _(step):
        goal = lax.rem(place + step, near)
        pltpu.make_async_remote_copy(
            src_ref=near_send.at[goal],
            dst_ref=near_recv.at[place],
            send_sem=near_sems.at[0],
            recv_sem=near_sems.at[1],
            device_id={"req": plane * near + goal},
            device_id_type=MESH,
        ).start()

    send_half(0)
    for head in range(EARLY_HEADS, HEADS):
        attend(head)

    def drain(ref, count, sem):
        span = ref.at[pl.ds(0, count)]
        pltpu.make_async_copy(span, span, sem).wait()

    drain(near_recv, near - 1, near_sems.at[1])
    for p in range(far):
        u = lax.rem(p * near + place + devices - turn, devices)
        far_send[p] = near_recv[lax.div(u, decodes)]

    @pl.loop(1, far)
    def _(step):
        goal = lax.rem(plane + step, far)
        pltpu.make_async_remote_copy(
            src_ref=far_send.at[goal],
            dst_ref=far_recv.at[plane],
            send_sem=far_sems.at[0],
            recv_sem=far_sems.at[1],
            device_id={"req": goal * near + place},
            device_id_type=MESH,
        ).start()

    send_half(1)

    kept = [
        pltpu.make_async_copy(
            send[side].at[devices - 1], recv[side].at[me], own_sems.at[side]
        )
        for side in range(2)
    ]
    kept.append(
        pltpu.make_async_copy(far_send.at[plane], far_recv.at[plane], own_sems.at[2])
    )
    for copy in kept:
        copy.start()
    for copy in kept:
        copy.wait()
    drain(near_send, near - 1, near_sems.at[0])
    drain(far_send, far - 1, far_sems.at[0])
    for side in range(2):
        drain(send[side], devices - 1, send_sems.at[side])

    token = lax.rem(me + devices - turn, devices)
    landing = jnp.sum(
        jnp.where(iota((even_rows, devices), 1) == token, regroup_ref[...], 0),
        axis=1,
        keepdims=True,
    ) - me * even_rows

    def lands(part):
        size = part.shape[0]
        diagonal = iota((size, size), 0) == iota((size, size), 1)
        row = jnp.sum(jnp.where(diagonal, part, 0), axis=0, keepdims=True)
        return (iota((even_rows, size), 0) == row).astype(F32).astype(BF16)

    diagonal = iota((devices, devices), 0) == iota((devices, devices), 1)
    owner = jnp.sum(jnp.where(diagonal, owner_ref[...], 0), axis=1, keepdims=True)
    came = (iota((devices, devices), 1) == owner).astype(F32).astype(BF16)
    pick = jnp.dot(
        lands(landing[:devices]), came, preferred_element_type=F32
    ).astype(BF16)
    pick_far = lands(landing[devices:])

    drain(far_recv, far - 1, far_sems.at[1])
    dec_wide[...] = far_recv[...].astype(F32)
    for c in range(chunks):
        dec_context[:, c * LANES : (c + 1) * LANES] = dec_wide[:, c, :]
    far_rows = jnp.dot(
        pick_far, dec_context[...].astype(BF16), preferred_element_type=F32
    )
    for side in range(2):
        span = spans[side]
        count = (span.stop - span.start) // LANES
        drain(recv[side], devices - 1, recv_sems.at[side])
        wide[:, :count, :] = recv[side][...].astype(F32)
        for c in range(count):
            low = span.start + c * LANES
            row = wide[:, c, :].astype(BF16)
            gathered_ref[:, low : low + LANES] = (
                jnp.dot(pick, row, preferred_element_type=F32)
                + far_rows[:, low : low + LANES]
            ).astype(BF16)


def finish_kernel(gathered_ref, residual_ref, gain_ref, sum_ref, norm_ref):
    width = residual_ref.shape[1]
    summed = residual_ref[...].astype(F32) + gathered_ref[...].astype(F32)
    inverse_rms = lax.rsqrt(jnp.mean(summed * summed, axis=1, keepdims=True) + norm_eps)
    sum_ref[...] = summed.astype(BF16)
    norm_ref[...] = (summed * inverse_rms * gain_ref[...].reshape(1, width)).astype(BF16)


def body(
    prefill_qkv,
    decode_qkv,
    conv_state,
    cache_len,
    page_table,
    page_pool,
    conv_taps,
    segment_owner,
    regroup,
    residual,
    norm_gain,
):
    devices = lax.axis_size("req")
    rows, _, width = prefill_qkv.shape
    decodes = decode_qkv.shape[0]
    even_rows = residual.shape[0]
    chunks = width // LANES
    near = devices // decodes
    table = regroup.reshape(regroup.shape[0] // devices, devices)
    owner = segment_owner.reshape(1, devices)
    smem = pl.BlockSpec(memory_space=pltpu.SMEM)
    vmem = pl.BlockSpec(memory_space=pltpu.VMEM)
    early = EARLY_LANES // LANES
    out = jax.ShapeDtypeStruct((even_rows, width), BF16)
    hbm = pl.BlockSpec(memory_space=pl.ANY)
    gathered = pl.pallas_call(
        functools.partial(exchange_kernel, devices, even_rows),
        out_shape=out,
        in_specs=[smem, smem, hbm] + [vmem] * 7,
        out_specs=vmem,
        scratch_shapes=[
            pltpu.VMEM((rows + 8, width), F32),
            pltpu.VMEM((PAGE + rows, width), BF16),
            pltpu.VMEM((PAGE + rows, width), BF16),
            pltpu.VMEM((rows, width), F32),
            pltpu.VMEM((decodes * HEADS, width), BF16),
            pltpu.VMEM((decodes * HEADS, width), F32),
            pltpu.VMEM(conv_state.shape, F32),
            pltpu.VMEM((decodes, width), F32),
            pltpu.VMEM((devices, early, LANES), F32),
            pltpu.VMEM((decodes, chunks, LANES), F32),
            pltpu.VMEM((devices, early, LANES), BF16),
            pltpu.VMEM((devices, chunks - early, LANES), BF16),
            pltpu.VMEM((devices, early, LANES), BF16),
            pltpu.VMEM((devices, chunks - early, LANES), BF16),
            pltpu.VMEM((decodes, chunks, LANES), BF16),
            pltpu.VMEM((decodes, chunks, LANES), BF16),
            pltpu.VMEM((near, chunks, LANES), BF16),
            pltpu.VMEM((near, chunks, LANES), BF16),
            pltpu.VMEM((decodes, chunks, LANES), BF16),
            pltpu.SemaphoreType.DMA((2,)),
            pltpu.SemaphoreType.DMA((2,)),
            pltpu.SemaphoreType.DMA((2,)),
            pltpu.SemaphoreType.DMA((2,)),
            pltpu.SemaphoreType.DMA((3,)),
            pltpu.SMEM((8, devices), I32),
        ],
        compiler_params=pltpu.CompilerParams(collective_id=0, has_side_effects=True),
        name="exchange",
    )(
        cache_len,
        page_table,
        table,
        prefill_qkv.transpose(1, 0, 2),
        decode_qkv.transpose(1, 0, 2),
        conv_state,
        page_pool,
        conv_taps,
        table,
        owner,
    )
    return pl.pallas_call(
        finish_kernel,
        out_shape=(out, out),
        in_specs=[vmem] * 3,
        out_specs=(vmem, vmem),
        name="finish",
    )(gathered, residual, norm_gain)


def solution(mesh):
    in_specs = (
        P(("rep", "req"), None, None),
        P(("rep", "req"), None, None),
        P(("rep", "req"), None, None),
        P(("rep", "req")),
        P(("rep", "req"), None),
        P(("rep", "req"), None, None, None),
        P(),
        P("rep"),
        P("rep"),
        P(("rep", "req"), None),
        P(),
    )
    out_specs = (P(("rep", "req"), None), P(("rep", "req"), None))
    return jax.shard_map(body, mesh=mesh, in_specs=in_specs, out_specs=out_specs, check_vma=False)
```

```python
import functools

import jax
import jax.numpy as jnp
from jax import lax
from jax.experimental import pallas as pl
from jax.experimental.pallas import tpu as pltpu
from jax.sharding import PartitionSpec as P

HEADS = 16
HEAD_CHANNELS = 112
WINDOW = 64
PAGE = 128
LANES = 128
EARLY_LANES = 1024
EARLY_HEADS = -(-EARLY_LANES // HEAD_CHANNELS)
MESH = pl.DeviceIdType.MESH

norm_eps = 1e-06
masked_score = -1e30
F32 = jnp.float32
BF16 = jnp.bfloat16
I32 = jnp.int32


def iota(shape, dim):
    return lax.broadcasted_iota(I32, shape, dim)


def dot_nt(a, b):
    return lax.dot_general(a, b, (((1,), (1,)), ((), ())), preferred_element_type=F32)


def offset_of(rank):
    return 4 + ((rank + 1) // 2) * (1 - 2 * (rank % 2))


def exchange_kernel(
    devices,
    even_rows,
    cache_len_ref,
    page_table_ref,
    table_ref,
    qkv_hbm,
    dqkv_hbm,
    state_hbm,
    pool_hbm,
    taps_hbm,
    regroup_hbm,
    owner_hbm,
    gathered_ref,
    extended,
    keys,
    values,
    context,
    dec_queries,
    dec_scores,
    state,
    dec_context,
    wide,
    dec_wide,
    send_0,
    send_1,
    recv_0,
    recv_1,
    far_recv,
    dec_rows,
    near_send,
    near_recv,
    far_send,
    send_sems,
    recv_sems,
    near_sems,
    far_sems,
    own_sems,
    head,
    qkv_ref,
    dqkv_ref,
    state_ref,
    pool_ref,
    taps_ref,
    regroup_ref,
    owner_ref,
    load_sems,
):
    me = lax.axis_index("req")
    rows = qkv_ref.shape[1]
    width = qkv_ref.shape[2]
    decodes = dqkv_ref.shape[1]
    chunks = width // LANES
    near = devices // decodes
    far = decodes
    place, plane = lax.rem(me, near), lax.div(me, near)
    column, core = lax.div(place, 2), lax.rem(place, 2)
    spans = [slice(0, EARLY_LANES), slice(EARLY_LANES, width)]
    scale = HEAD_CHANNELS ** (-0.5)
    first = pltpu.make_async_copy(
        table_ref.at[pl.ds(0, 8)], head, own_sems.at[0]
    )
    first.start()
    loads = [
        pltpu.make_async_copy(source, target, load_sems.at[n])
        for n, (source, target) in enumerate(
            [
                (dqkv_hbm, dqkv_ref),
                (state_hbm, state_ref),
                (taps_hbm, taps_ref),
                (pool_hbm, pool_ref),
                (qkv_hbm, qkv_ref),
                (regroup_hbm, regroup_ref),
                (owner_hbm, owner_ref),
            ]
        )
    ]
    for load in loads:
        load.start()

    send, recv = (send_0, send_1), (recv_0, recv_1)
    barrier = pltpu.get_barrier_semaphore()

    def greet(step):
        pl.semaphore_signal(
            barrier,
            inc=1,
            device_id={"req": lax.rem(me + step, devices)},
            device_id_type=MESH,
        )

    pl.loop(devices // 2, devices)(greet)
    pl.loop(1, devices // 2)(greet)

    def cached_positions(r, shape, dim):
        cached = cache_len_ref[r]
        top = jnp.maximum((cached - 1) >> 7, 0)
        below = jnp.maximum(top - 1, 0)
        at_top, at_below = page_table_ref[r, top], page_table_ref[r, below]
        offset = iota(shape, dim)
        position = cached - 1 - ((cached - 1 - offset) & (PAGE - 1))
        page = jnp.where(position >= top * PAGE, at_top, at_below)
        return cached, position, page

    for load in loads[:4]:
        load.wait()
    state[...] = state_ref[...].astype(F32)

    first.wait()
    turn = lax.div(head[0, 0], even_rows)
    lane = iota((HEADS, width), 1)
    low = iota((HEADS, width), 0) * HEAD_CHANNELS
    mine = (lane >= low) & (lane < low + HEAD_CHANNELS)
    fresh = (
        taps_ref[0:1, :] * state[1 : 1 + decodes, 0, :]
        + taps_ref[1:2, :] * state[1 : 1 + decodes, 1, :]
        + taps_ref[2:3, :] * dqkv_ref[1].astype(F32)
    ).astype(BF16).astype(F32)
    queries = dqkv_ref[0].astype(F32)
    new_values = dqkv_ref[2].astype(F32)
    own = []
    bias_rows = []
    for r in range(decodes):
        spread = jnp.where(mine, queries[r : r + 1, :], 0.0)
        dec_queries[r * HEADS : (r + 1) * HEADS, :] = spread.astype(BF16)
        own.append(jnp.sum(spread * fresh[r : r + 1, :], axis=1, keepdims=True))
        cached, position, page = cached_positions(1 + r, (HEADS, PAGE), 1)
        ok = (position >= 0) & (position >= cached - (WINDOW - 1))
        bias_rows.append(
            jnp.concatenate(
                [
                    jnp.where(ok & (page == n), 0.0, masked_score).astype(F32)
                    for n in range(2)
                ],
                axis=1,
            )
        )
    own = jnp.concatenate(own, axis=0) * scale
    scores = jnp.concatenate(
        [dot_nt(dec_queries[...], pool_ref[n, 0]) for n in range(2)], axis=1
    )
    scores = scores * scale + jnp.concatenate(bias_rows, axis=0)
    top = jnp.maximum(jnp.max(scores, axis=1, keepdims=True), own)
    raised = jnp.exp(scores - top)
    own = jnp.exp(own - top)
    total = 1.0 / (jnp.sum(raised, axis=1, keepdims=True) + own)
    weights = (raised * total).astype(BF16)
    own = (own * total).astype(BF16).astype(F32)
    dec_scores[...] = jnp.dot(
        weights[:, :PAGE], pool_ref[0, 1], preferred_element_type=F32
    ) + jnp.dot(weights[:, PAGE:], pool_ref[1, 1], preferred_element_type=F32)
    for r in range(decodes):
        span = slice(r * HEADS, (r + 1) * HEADS)
        mixed = dec_scores[span, :] + own[span, :] * new_values[r : r + 1, :]
        dec_context[r : r + 1, :] = jnp.sum(
            jnp.where(mine, mixed, 0.0), axis=0, keepdims=True
        )
    for c in range(chunks):
        dec_wide[:, c, :] = dec_context[:, c * LANES : (c + 1) * LANES]
    dec_rows[...] = dec_wide[...].astype(BF16)
    for p in range(near):
        j = lax.rem(p + 2 * devices - turn - decodes * lax.rem(me, 2), near)
        near_send[p] = dec_rows[jnp.minimum(j, decodes - 1)]

    loads[4].wait()
    _, _, page = cached_positions(0, (PAGE, width), 0)
    first_page = page == 0
    keys[0:PAGE, :] = jnp.where(
        first_page, pool_ref[0, 0].astype(F32), pool_ref[1, 0].astype(F32)
    ).astype(BF16)
    values[0:PAGE, :] = jnp.where(
        first_page, pool_ref[0, 1].astype(F32), pool_ref[1, 1].astype(F32)
    ).astype(BF16)
    extended[6:8, :] = state[0]
    extended[8 : 8 + rows, :] = qkv_ref[1].astype(F32)
    keys[PAGE : PAGE + rows, :] = (
        taps_ref[0:1, :] * extended[6 : 6 + rows, :]
        + taps_ref[1:2, :] * extended[7 : 7 + rows, :]
        + taps_ref[2:3, :] * extended[8 : 8 + rows, :]
    ).astype(BF16)
    values[PAGE : PAGE + rows, :] = qkv_ref[2]

    def fresh_bias(begin, count):
        other = iota((WINDOW, count), 1)
        token = iota((WINDOW, count), 0) + begin
        ok = (other <= token) & (other >= token - (WINDOW - 1))
        return jnp.where(ok, 0.0, masked_score).astype(F32)

    cached, position, _ = cached_positions(0, (WINDOW, PAGE), 1)
    token = iota((WINDOW, PAGE), 0)
    ok = (position >= 0) & (position >= cached + token - (WINDOW - 1))
    bands = [
        (
            0,
            0,
            PAGE + WINDOW,
            jnp.concatenate(
                [jnp.where(ok, 0.0, masked_score).astype(F32), fresh_bias(0, WINDOW)],
                axis=1,
            ),
        )
    ]
    for begin in range(WINDOW, rows, WINDOW):
        first_key = begin - WINDOW
        bands.append((begin, PAGE + first_key, 2 * WINDOW, fresh_bias(WINDOW, 2 * WINDOW)))
    context[...] = jnp.zeros_like(context)

    def attend(head):
        low, high = head * HEAD_CHANNELS, (head + 1) * HEAD_CHANNELS
        start = low // LANES * LANES
        stop = -(-high // LANES) * LANES
        lane = iota((WINDOW, stop - start), 1) + start
        mine = (lane >= low) & (lane < high)
        for begin, key, count, bias in bands:
            block = slice(begin, begin + WINDOW)
            query = qkv_ref[0, block, start:stop].astype(F32)
            query = jnp.where(mine, query, 0.0).astype(BF16)
            scores = dot_nt(query, keys[key : key + count, start:stop]) * scale + bias
            top = jnp.max(scores, axis=1, keepdims=True)
            raised = jnp.exp(scores - top)
            share = 1.0 / jnp.sum(raised, axis=1, keepdims=True)
            part = jnp.dot(
                (raised * share).astype(BF16),
                values[key : key + count, start:stop],
                preferred_element_type=F32,
            )
            context[block, start:stop] = jnp.where(mine, part, context[block, start:stop])

    slot = iota((devices, rows), 0)

    def offsets(rank):
        return 4 + ((rank + 1) >> 1) * (1 - 2 * (rank & 1))

    target = (
        ((plane + offsets(slot >> 4)) & (far - 1)) * near
        + ((column + offsets((slot >> 1) & 7)) & 7) * 2
        + ((core + 1 + slot) & 1)
    )
    chosen = ((target - turn) & (devices - 1)) == iota((devices, rows), 1)
    chosen = chosen.astype(F32).astype(BF16)

    def send_half(side):
        span = spans[side]
        sent = jnp.dot(
            chosen, context[:, span].astype(BF16), preferred_element_type=F32
        )
        count = (span.stop - span.start) // LANES
        for c in range(count):
            wide[:, c, :] = sent[:, c * LANES : (c + 1) * LANES]
        send[side][...] = wide[:, :count, :].astype(BF16)

        def to_chip(rank_z, rank_y, cores):
            goal_z = lax.rem(plane + offset_of(rank_z), far)
            goal_y = lax.rem(column + offset_of(rank_y), 8)
            for c in range(cores):
                goal_core = lax.rem(core + 1 + c, 2)
                pltpu.make_async_remote_copy(
                    src_ref=send[side].at[(rank_z * 8 + rank_y) * 2 + c],
                    dst_ref=recv[side].at[me],
                    send_sem=send_sems.at[side],
                    recv_sem=recv_sems.at[side],
                    device_id={"req": goal_z * near + goal_y * 2 + goal_core},
                    device_id_type=MESH,
                ).start()

        for shell in range(far):
            for rank in range(shell):
                to_chip(shell, rank, 2)
                to_chip(rank, shell, 2)
            to_chip(shell, shell, 2 if shell < far - 1 else 1)

    for head in range(EARLY_HEADS):
        attend(head)

    pl.semaphore_wait(barrier, devices - 1)

    near_recv[place] = near_send[place]

    @pl.loop(1, near)
    def _(step):
        goal = lax.rem(place + step, near)
        pltpu.make_async_remote_copy(
            src_ref=near_send.at[goal],
            dst_ref=near_recv.at[place],
            send_sem=near_sems.at[0],
            recv_sem=near_sems.at[1],
            device_id={"req": plane * near + goal},
            device_id_type=MESH,
        ).start()

    send_half(0)
    for head in range(EARLY_HEADS, HEADS):
        attend(head)

    def drain(ref, count, sem):
        span = ref.at[pl.ds(0, count)]
        pltpu.make_async_copy(span, span, sem).wait()

    drain(near_recv, near - 1, near_sems.at[1])
    for p in range(far):
        u = lax.rem(p * near + place + devices - turn, devices)
        far_send[p] = near_recv[lax.div(u, decodes)]

    @pl.loop(1, far)
    def _(step):
        goal = lax.rem(plane + step, far)
        pltpu.make_async_remote_copy(
            src_ref=far_send.at[goal],
            dst_ref=far_recv.at[plane],
            send_sem=far_sems.at[0],
            recv_sem=far_sems.at[1],
            device_id={"req": goal * near + place},
            device_id_type=MESH,
        ).start()

    send_half(1)

    kept = [
        pltpu.make_async_copy(
            send[side].at[devices - 1], recv[side].at[me], own_sems.at[side]
        )
        for side in range(2)
    ]
    kept.append(
        pltpu.make_async_copy(far_send.at[plane], far_recv.at[plane], own_sems.at[2])
    )
    for copy in kept:
        copy.start()
    for copy in kept:
        copy.wait()
    drain(near_send, near - 1, near_sems.at[0])
    drain(far_send, far - 1, far_sems.at[0])
    for side in range(2):
        drain(send[side], devices - 1, send_sems.at[side])

    loads[5].wait()
    loads[6].wait()
    token = lax.rem(me + devices - turn, devices)
    landing = jnp.sum(
        jnp.where(iota((even_rows, devices), 1) == token, regroup_ref[...], 0),
        axis=1,
        keepdims=True,
    ) - me * even_rows

    def lands(part):
        size = part.shape[0]
        diagonal = iota((size, size), 0) == iota((size, size), 1)
        row = jnp.sum(jnp.where(diagonal, part, 0), axis=0, keepdims=True)
        return (iota((even_rows, size), 0) == row).astype(F32).astype(BF16)

    diagonal = iota((devices, devices), 0) == iota((devices, devices), 1)
    owner = jnp.sum(jnp.where(diagonal, owner_ref[...], 0), axis=1, keepdims=True)
    came = (iota((devices, devices), 1) == owner).astype(F32).astype(BF16)
    pick = jnp.dot(
        lands(landing[:devices]), came, preferred_element_type=F32
    ).astype(BF16)
    pick_far = lands(landing[devices:])

    drain(far_recv, far - 1, far_sems.at[1])
    dec_wide[...] = far_recv[...].astype(F32)
    for c in range(chunks):
        dec_context[:, c * LANES : (c + 1) * LANES] = dec_wide[:, c, :]
    far_rows = jnp.dot(
        pick_far, dec_context[...].astype(BF16), preferred_element_type=F32
    )
    for side in range(2):
        span = spans[side]
        count = (span.stop - span.start) // LANES
        drain(recv[side], devices - 1, recv_sems.at[side])
        wide[:, :count, :] = recv[side][...].astype(F32)
        for c in range(count):
            low = span.start + c * LANES
            row = wide[:, c, :].astype(BF16)
            gathered_ref[:, low : low + LANES] = (
                jnp.dot(pick, row, preferred_element_type=F32)
                + far_rows[:, low : low + LANES]
            ).astype(BF16)


def finish_kernel(gathered_ref, residual_ref, gain_ref, sum_ref, norm_ref):
    width = residual_ref.shape[1]
    summed = residual_ref[...].astype(F32) + gathered_ref[...].astype(F32)
    inverse_rms = lax.rsqrt(jnp.mean(summed * summed, axis=1, keepdims=True) + norm_eps)
    sum_ref[...] = summed.astype(BF16)
    norm_ref[...] = (summed * inverse_rms * gain_ref[...].reshape(1, width)).astype(BF16)


def body(
    prefill_qkv,
    decode_qkv,
    conv_state,
    cache_len,
    page_table,
    page_pool,
    conv_taps,
    segment_owner,
    regroup,
    residual,
    norm_gain,
):
    devices = lax.axis_size("req")
    rows, _, width = prefill_qkv.shape
    decodes = decode_qkv.shape[0]
    even_rows = residual.shape[0]
    chunks = width // LANES
    near = devices // decodes
    table = regroup.reshape(regroup.shape[0] // devices, devices)
    owner = segment_owner.reshape(1, devices)
    smem = pl.BlockSpec(memory_space=pltpu.SMEM)
    vmem = pl.BlockSpec(memory_space=pltpu.VMEM)
    early = EARLY_LANES // LANES
    out = jax.ShapeDtypeStruct((even_rows, width), BF16)
    hbm = pl.BlockSpec(memory_space=pl.ANY)
    gathered = pl.pallas_call(
        functools.partial(exchange_kernel, devices, even_rows),
        out_shape=out,
        in_specs=[smem, smem] + [hbm] * 8,
        out_specs=vmem,
        scratch_shapes=[
            pltpu.VMEM((rows + 8, width), F32),
            pltpu.VMEM((PAGE + rows, width), BF16),
            pltpu.VMEM((PAGE + rows, width), BF16),
            pltpu.VMEM((rows, width), F32),
            pltpu.VMEM((decodes * HEADS, width), BF16),
            pltpu.VMEM((decodes * HEADS, width), F32),
            pltpu.VMEM(conv_state.shape, F32),
            pltpu.VMEM((decodes, width), F32),
            pltpu.VMEM((devices, early, LANES), F32),
            pltpu.VMEM((decodes, chunks, LANES), F32),
            pltpu.VMEM((devices, early, LANES), BF16),
            pltpu.VMEM((devices, chunks - early, LANES), BF16),
            pltpu.VMEM((devices, early, LANES), BF16),
            pltpu.VMEM((devices, chunks - early, LANES), BF16),
            pltpu.VMEM((decodes, chunks, LANES), BF16),
            pltpu.VMEM((decodes, chunks, LANES), BF16),
            pltpu.VMEM((near, chunks, LANES), BF16),
            pltpu.VMEM((near, chunks, LANES), BF16),
            pltpu.VMEM((decodes, chunks, LANES), BF16),
            pltpu.SemaphoreType.DMA((2,)),
            pltpu.SemaphoreType.DMA((2,)),
            pltpu.SemaphoreType.DMA((2,)),
            pltpu.SemaphoreType.DMA((2,)),
            pltpu.SemaphoreType.DMA((3,)),
            pltpu.SMEM((8, devices), I32),
            pltpu.VMEM((3, rows, width), BF16),
            pltpu.VMEM((3, decodes, width), BF16),
            pltpu.VMEM(conv_state.shape, BF16),
            pltpu.VMEM(page_pool.shape, BF16),
            pltpu.VMEM(conv_taps.shape, F32),
            pltpu.VMEM(table.shape, I32),
            pltpu.VMEM(owner.shape, I32),
            pltpu.SemaphoreType.DMA((7,)),
        ],
        compiler_params=pltpu.CompilerParams(collective_id=0, has_side_effects=True),
        name="exchange",
    )(
        cache_len,
        page_table,
        table,
        prefill_qkv.transpose(1, 0, 2),
        decode_qkv.transpose(1, 0, 2),
        conv_state,
        page_pool,
        conv_taps,
        table,
        owner,
    )
    return pl.pallas_call(
        finish_kernel,
        out_shape=(out, out),
        in_specs=[vmem] * 3,
        out_specs=(vmem, vmem),
        name="finish",
    )(gathered, residual, norm_gain)


def solution(mesh):
    in_specs = (
        P(("rep", "req"), None, None),
        P(("rep", "req"), None, None),
        P(("rep", "req"), None, None),
        P(("rep", "req")),
        P(("rep", "req"), None),
        P(("rep", "req"), None, None, None),
        P(),
        P("rep"),
        P("rep"),
        P(("rep", "req"), None),
        P(),
    )
    out_specs = (P(("rep", "req"), None), P(("rep", "req"), None))
    return jax.shard_map(body, mesh=mesh, in_specs=in_specs, out_specs=out_specs, check_vma=False)
```

```python
import functools

import jax
import jax.numpy as jnp
from jax import lax
from jax.experimental import pallas as pl
from jax.experimental.pallas import tpu as pltpu
from jax.sharding import PartitionSpec as P

HEADS = 16
HEAD_CHANNELS = 112
WINDOW = 64
PAGE = 128
LANES = 128
EARLY_LANES = 1024
EARLY_HEADS = -(-EARLY_LANES // HEAD_CHANNELS)
MESH = pl.DeviceIdType.MESH

norm_eps = 1e-06
masked_score = -1e30
F32 = jnp.float32
BF16 = jnp.bfloat16
I32 = jnp.int32


def iota(shape, dim):
    return lax.broadcasted_iota(I32, shape, dim)


def dot_nt(a, b):
    return lax.dot_general(a, b, (((1,), (1,)), ((), ())), preferred_element_type=F32)


def chip_offsets(side):
    reach = side // 2
    pairs = [(a, b) for a in range(reach + 1) for b in range(reach + 1)]
    pairs.sort(key=lambda pair: (-sum(pair), pair))
    steps = []
    for a, b in pairs:
        for step in ((a, b), (-a, -b), (a, -b), (-a, b)):
            step = (step[0] % side, step[1] % side)
            if step not in steps:
                steps.append(step)
    return steps


def exchange_kernel(
    devices,
    even_rows,
    cache_len_ref,
    page_table_ref,
    table_ref,
    qkv_hbm,
    dqkv_hbm,
    state_hbm,
    pool_hbm,
    taps_hbm,
    regroup_hbm,
    owner_hbm,
    gathered_ref,
    extended,
    keys,
    values,
    context,
    dec_queries,
    dec_scores,
    state,
    dec_context,
    wide,
    dec_wide,
    send_0,
    send_1,
    recv_0,
    recv_1,
    far_recv,
    dec_rows,
    near_send,
    near_recv,
    far_send,
    send_sems,
    recv_sems,
    near_sems,
    far_sems,
    own_sems,
    head,
    qkv_ref,
    dqkv_ref,
    state_ref,
    pool_ref,
    taps_ref,
    regroup_ref,
    owner_ref,
    load_sems,
):
    me = lax.axis_index("req")
    rows = qkv_ref.shape[1]
    width = qkv_ref.shape[2]
    decodes = dqkv_ref.shape[1]
    chunks = width // LANES
    near = devices // decodes
    far = decodes
    place, plane = lax.rem(me, near), lax.div(me, near)
    column, core = lax.div(place, 2), lax.rem(place, 2)
    spans = [slice(0, EARLY_LANES), slice(EARLY_LANES, width)]
    scale = HEAD_CHANNELS ** (-0.5)
    first = pltpu.make_async_copy(
        table_ref.at[pl.ds(0, 8)], head, own_sems.at[0]
    )
    first.start()
    loads = [
        pltpu.make_async_copy(source, target, load_sems.at[n])
        for n, (source, target) in enumerate(
            [
                (dqkv_hbm, dqkv_ref),
                (state_hbm, state_ref),
                (taps_hbm, taps_ref),
                (pool_hbm, pool_ref),
                (qkv_hbm, qkv_ref),
                (regroup_hbm, regroup_ref),
                (owner_hbm, owner_ref),
            ]
        )
    ]
    for load in loads:
        load.start()

    send, recv = (send_0, send_1), (recv_0, recv_1)
    barrier = pltpu.get_barrier_semaphore()

    def greet(step):
        pl.semaphore_signal(
            barrier,
            inc=1,
            device_id={"req": lax.rem(me + step, devices)},
            device_id_type=MESH,
        )

    pl.loop(devices // 2, devices)(greet)
    pl.loop(1, devices // 2)(greet)

    def cached_positions(r, shape, dim):
        cached = cache_len_ref[r]
        top = jnp.maximum((cached - 1) >> 7, 0)
        below = jnp.maximum(top - 1, 0)
        at_top, at_below = page_table_ref[r, top], page_table_ref[r, below]
        offset = iota(shape, dim)
        position = cached - 1 - ((cached - 1 - offset) & (PAGE - 1))
        page = jnp.where(position >= top * PAGE, at_top, at_below)
        return cached, position, page

    for load in loads[:4]:
        load.wait()
    state[...] = state_ref[...].astype(F32)

    first.wait()
    turn = lax.div(head[0, 0], even_rows)
    lane = iota((HEADS, width), 1)
    low = iota((HEADS, width), 0) * HEAD_CHANNELS
    mine = (lane >= low) & (lane < low + HEAD_CHANNELS)
    fresh = (
        taps_ref[0:1, :] * state[1 : 1 + decodes, 0, :]
        + taps_ref[1:2, :] * state[1 : 1 + decodes, 1, :]
        + taps_ref[2:3, :] * dqkv_ref[1].astype(F32)
    ).astype(BF16).astype(F32)
    queries = dqkv_ref[0].astype(F32)
    new_values = dqkv_ref[2].astype(F32)
    own = []
    bias_rows = []
    for r in range(decodes):
        spread = jnp.where(mine, queries[r : r + 1, :], 0.0)
        dec_queries[r * HEADS : (r + 1) * HEADS, :] = spread.astype(BF16)
        own.append(jnp.sum(spread * fresh[r : r + 1, :], axis=1, keepdims=True))
        cached, position, page = cached_positions(1 + r, (HEADS, PAGE), 1)
        ok = (position >= 0) & (position >= cached - (WINDOW - 1))
        bias_rows.append(
            jnp.concatenate(
                [
                    jnp.where(ok & (page == n), 0.0, masked_score).astype(F32)
                    for n in range(2)
                ],
                axis=1,
            )
        )
    own = jnp.concatenate(own, axis=0) * scale
    scores = jnp.concatenate(
        [dot_nt(dec_queries[...], pool_ref[n, 0]) for n in range(2)], axis=1
    )
    scores = scores * scale + jnp.concatenate(bias_rows, axis=0)
    top = jnp.maximum(jnp.max(scores, axis=1, keepdims=True), own)
    raised = jnp.exp(scores - top)
    own = jnp.exp(own - top)
    total = 1.0 / (jnp.sum(raised, axis=1, keepdims=True) + own)
    weights = (raised * total).astype(BF16)
    own = (own * total).astype(BF16).astype(F32)
    dec_scores[...] = jnp.dot(
        weights[:, :PAGE], pool_ref[0, 1], preferred_element_type=F32
    ) + jnp.dot(weights[:, PAGE:], pool_ref[1, 1], preferred_element_type=F32)
    for r in range(decodes):
        span = slice(r * HEADS, (r + 1) * HEADS)
        mixed = dec_scores[span, :] + own[span, :] * new_values[r : r + 1, :]
        dec_context[r : r + 1, :] = jnp.sum(
            jnp.where(mine, mixed, 0.0), axis=0, keepdims=True
        )
    for c in range(chunks):
        dec_wide[:, c, :] = dec_context[:, c * LANES : (c + 1) * LANES]
    dec_rows[...] = dec_wide[...].astype(BF16)
    for p in range(near):
        j = lax.rem(p + 2 * devices - turn - decodes * lax.rem(me, 2), near)
        near_send[p] = dec_rows[jnp.minimum(j, decodes - 1)]

    loads[4].wait()
    _, _, page = cached_positions(0, (PAGE, width), 0)
    first_page = page == 0
    keys[0:PAGE, :] = jnp.where(
        first_page, pool_ref[0, 0].astype(F32), pool_ref[1, 0].astype(F32)
    ).astype(BF16)
    values[0:PAGE, :] = jnp.where(
        first_page, pool_ref[0, 1].astype(F32), pool_ref[1, 1].astype(F32)
    ).astype(BF16)
    extended[6:8, :] = state[0]
    extended[8 : 8 + rows, :] = qkv_ref[1].astype(F32)
    keys[PAGE : PAGE + rows, :] = (
        taps_ref[0:1, :] * extended[6 : 6 + rows, :]
        + taps_ref[1:2, :] * extended[7 : 7 + rows, :]
        + taps_ref[2:3, :] * extended[8 : 8 + rows, :]
    ).astype(BF16)
    values[PAGE : PAGE + rows, :] = qkv_ref[2]

    def fresh_bias(begin, count):
        other = iota((WINDOW, count), 1)
        token = iota((WINDOW, count), 0) + begin
        ok = (other <= token) & (other >= token - (WINDOW - 1))
        return jnp.where(ok, 0.0, masked_score).astype(F32)

    cached, position, _ = cached_positions(0, (WINDOW, PAGE), 1)
    token = iota((WINDOW, PAGE), 0)
    ok = (position >= 0) & (position >= cached + token - (WINDOW - 1))
    bands = [
        (
            0,
            0,
            PAGE + WINDOW,
            jnp.concatenate(
                [jnp.where(ok, 0.0, masked_score).astype(F32), fresh_bias(0, WINDOW)],
                axis=1,
            ),
        )
    ]
    for begin in range(WINDOW, rows, WINDOW):
        first_key = begin - WINDOW
        bands.append((begin, PAGE + first_key, 2 * WINDOW, fresh_bias(WINDOW, 2 * WINDOW)))
    context[...] = jnp.zeros_like(context)

    def attend(head):
        low, high = head * HEAD_CHANNELS, (head + 1) * HEAD_CHANNELS
        start = low // LANES * LANES
        stop = -(-high // LANES) * LANES
        lane = iota((WINDOW, stop - start), 1) + start
        mine = (lane >= low) & (lane < high)
        for begin, key, count, bias in bands:
            block = slice(begin, begin + WINDOW)
            query = qkv_ref[0, block, start:stop].astype(F32)
            query = jnp.where(mine, query, 0.0).astype(BF16)
            scores = dot_nt(query, keys[key : key + count, start:stop]) * scale + bias
            top = jnp.max(scores, axis=1, keepdims=True)
            raised = jnp.exp(scores - top)
            share = 1.0 / jnp.sum(raised, axis=1, keepdims=True)
            part = jnp.dot(
                (raised * share).astype(BF16),
                values[key : key + count, start:stop],
                preferred_element_type=F32,
            )
            context[block, start:stop] = jnp.where(mine, part, context[block, start:stop])

    slot = iota((devices, rows), 0)

    turning = 1 - 2 * core
    target = (
        ((plane + far + turning * (slot >> 4)) & (far - 1)) * near
        + ((column + far + turning * ((slot >> 1) & 7)) & 7) * 2
        + ((core + 1 + slot) & 1)
    )
    chosen = ((target - turn) & (devices - 1)) == iota((devices, rows), 1)
    chosen = chosen.astype(F32).astype(BF16)

    def send_half(side):
        span = spans[side]
        sent = jnp.dot(
            chosen, context[:, span].astype(BF16), preferred_element_type=F32
        )
        count = (span.stop - span.start) // LANES
        for c in range(count):
            wide[:, c, :] = sent[:, c * LANES : (c + 1) * LANES]
        send[side][...] = wide[:, :count, :].astype(BF16)

        for step_z, step_y in chip_offsets(far):
            goal_z = lax.rem(plane + far + turning * step_z, far)
            goal_y = lax.rem(column + far + turning * step_y, far)
            for c in range(2 if step_z or step_y else 1):
                goal_core = lax.rem(core + 1 + c, 2)
                pltpu.make_async_remote_copy(
                    src_ref=send[side].at[(step_z * far + step_y) * 2 + c],
                    dst_ref=recv[side].at[me],
                    send_sem=send_sems.at[side],
                    recv_sem=recv_sems.at[side],
                    device_id={"req": goal_z * near + goal_y * 2 + goal_core},
                    device_id_type=MESH,
                ).start()

    for head in range(EARLY_HEADS):
        attend(head)

    pl.semaphore_wait(barrier, devices - 1)

    near_recv[place] = near_send[place]

    @pl.loop(1, near)
    def _(step):
        goal = lax.rem(place + step, near)
        pltpu.make_async_remote_copy(
            src_ref=near_send.at[goal],
            dst_ref=near_recv.at[place],
            send_sem=near_sems.at[0],
            recv_sem=near_sems.at[1],
            device_id={"req": plane * near + goal},
            device_id_type=MESH,
        ).start()

    send_half(0)
    for head in range(EARLY_HEADS, HEADS):
        attend(head)

    def drain(ref, count, sem):
        span = ref.at[pl.ds(0, count)]
        pltpu.make_async_copy(span, span, sem).wait()

    drain(near_recv, near - 1, near_sems.at[1])
    for p in range(far):
        u = lax.rem(p * near + place + devices - turn, devices)
        far_send[p] = near_recv[lax.div(u, decodes)]

    @pl.loop(1, far)
    def _(step):
        goal = lax.rem(plane + step, far)
        pltpu.make_async_remote_copy(
            src_ref=far_send.at[goal],
            dst_ref=far_recv.at[plane],
            send_sem=far_sems.at[0],
            recv_sem=far_sems.at[1],
            device_id={"req": goal * near + place},
            device_id_type=MESH,
        ).start()

    send_half(1)

    kept = [
        pltpu.make_async_copy(
            send[side].at[1], recv[side].at[me], own_sems.at[side]
        )
        for side in range(2)
    ]
    kept.append(
        pltpu.make_async_copy(far_send.at[plane], far_recv.at[plane], own_sems.at[2])
    )
    for copy in kept:
        copy.start()
    for copy in kept:
        copy.wait()
    drain(near_send, near - 1, near_sems.at[0])
    drain(far_send, far - 1, far_sems.at[0])
    for side in range(2):
        drain(send[side], devices - 1, send_sems.at[side])

    loads[5].wait()
    loads[6].wait()
    token = lax.rem(me + devices - turn, devices)
    landing = jnp.sum(
        jnp.where(iota((even_rows, devices), 1) == token, regroup_ref[...], 0),
        axis=1,
        keepdims=True,
    ) - me * even_rows

    def lands(part):
        size = part.shape[0]
        diagonal = iota((size, size), 0) == iota((size, size), 1)
        row = jnp.sum(jnp.where(diagonal, part, 0), axis=0, keepdims=True)
        return (iota((even_rows, size), 0) == row).astype(F32).astype(BF16)

    diagonal = iota((devices, devices), 0) == iota((devices, devices), 1)
    owner = jnp.sum(jnp.where(diagonal, owner_ref[...], 0), axis=1, keepdims=True)
    came = (iota((devices, devices), 1) == owner).astype(F32).astype(BF16)
    pick = jnp.dot(
        lands(landing[:devices]), came, preferred_element_type=F32
    ).astype(BF16)
    pick_far = lands(landing[devices:])

    drain(far_recv, far - 1, far_sems.at[1])
    dec_wide[...] = far_recv[...].astype(F32)
    for c in range(chunks):
        dec_context[:, c * LANES : (c + 1) * LANES] = dec_wide[:, c, :]
    far_rows = jnp.dot(
        pick_far, dec_context[...].astype(BF16), preferred_element_type=F32
    )
    for side in range(2):
        span = spans[side]
        count = (span.stop - span.start) // LANES
        drain(recv[side], devices - 1, recv_sems.at[side])
        wide[:, :count, :] = recv[side][...].astype(F32)
        for c in range(count):
            low = span.start + c * LANES
            row = wide[:, c, :].astype(BF16)
            gathered_ref[:, low : low + LANES] = (
                jnp.dot(pick, row, preferred_element_type=F32)
                + far_rows[:, low : low + LANES]
            ).astype(BF16)


def finish_kernel(gathered_ref, residual_ref, gain_ref, sum_ref, norm_ref):
    width = residual_ref.shape[1]
    summed = residual_ref[...].astype(F32) + gathered_ref[...].astype(F32)
    inverse_rms = lax.rsqrt(jnp.mean(summed * summed, axis=1, keepdims=True) + norm_eps)
    sum_ref[...] = summed.astype(BF16)
    norm_ref[...] = (summed * inverse_rms * gain_ref[...].reshape(1, width)).astype(BF16)


def body(
    prefill_qkv,
    decode_qkv,
    conv_state,
    cache_len,
    page_table,
    page_pool,
    conv_taps,
    segment_owner,
    regroup,
    residual,
    norm_gain,
):
    devices = lax.axis_size("req")
    rows, _, width = prefill_qkv.shape
    decodes = decode_qkv.shape[0]
    even_rows = residual.shape[0]
    chunks = width // LANES
    near = devices // decodes
    table = regroup.reshape(regroup.shape[0] // devices, devices)
    owner = segment_owner.reshape(1, devices)
    smem = pl.BlockSpec(memory_space=pltpu.SMEM)
    vmem = pl.BlockSpec(memory_space=pltpu.VMEM)
    early = EARLY_LANES // LANES
    out = jax.ShapeDtypeStruct((even_rows, width), BF16)
    hbm = pl.BlockSpec(memory_space=pl.ANY)
    gathered = pl.pallas_call(
        functools.partial(exchange_kernel, devices, even_rows),
        out_shape=out,
        in_specs=[smem, smem] + [hbm] * 8,
        out_specs=vmem,
        scratch_shapes=[
            pltpu.VMEM((rows + 8, width), F32),
            pltpu.VMEM((PAGE + rows, width), BF16),
            pltpu.VMEM((PAGE + rows, width), BF16),
            pltpu.VMEM((rows, width), F32),
            pltpu.VMEM((decodes * HEADS, width), BF16),
            pltpu.VMEM((decodes * HEADS, width), F32),
            pltpu.VMEM(conv_state.shape, F32),
            pltpu.VMEM((decodes, width), F32),
            pltpu.VMEM((devices, early, LANES), F32),
            pltpu.VMEM((decodes, chunks, LANES), F32),
            pltpu.VMEM((devices, early, LANES), BF16),
            pltpu.VMEM((devices, chunks - early, LANES), BF16),
            pltpu.VMEM((devices, early, LANES), BF16),
            pltpu.VMEM((devices, chunks - early, LANES), BF16),
            pltpu.VMEM((decodes, chunks, LANES), BF16),
            pltpu.VMEM((decodes, chunks, LANES), BF16),
            pltpu.VMEM((near, chunks, LANES), BF16),
            pltpu.VMEM((near, chunks, LANES), BF16),
            pltpu.VMEM((decodes, chunks, LANES), BF16),
            pltpu.SemaphoreType.DMA((2,)),
            pltpu.SemaphoreType.DMA((2,)),
            pltpu.SemaphoreType.DMA((2,)),
            pltpu.SemaphoreType.DMA((2,)),
            pltpu.SemaphoreType.DMA((3,)),
            pltpu.SMEM((8, devices), I32),
            pltpu.VMEM((3, rows, width), BF16),
            pltpu.VMEM((3, decodes, width), BF16),
            pltpu.VMEM(conv_state.shape, BF16),
            pltpu.VMEM(page_pool.shape, BF16),
            pltpu.VMEM(conv_taps.shape, F32),
            pltpu.VMEM(table.shape, I32),
            pltpu.VMEM(owner.shape, I32),
            pltpu.SemaphoreType.DMA((7,)),
        ],
        compiler_params=pltpu.CompilerParams(collective_id=0, has_side_effects=True),
        name="exchange",
    )(
        cache_len,
        page_table,
        table,
        prefill_qkv.transpose(1, 0, 2),
        decode_qkv.transpose(1, 0, 2),
        conv_state,
        page_pool,
        conv_taps,
        table,
        owner,
    )
    return pl.pallas_call(
        finish_kernel,
        out_shape=(out, out),
        in_specs=[vmem] * 3,
        out_specs=(vmem, vmem),
        name="finish",
    )(gathered, residual, norm_gain)


def solution(mesh):
    in_specs = (
        P(("rep", "req"), None, None),
        P(("rep", "req"), None, None),
        P(("rep", "req"), None, None),
        P(("rep", "req")),
        P(("rep", "req"), None),
        P(("rep", "req"), None, None, None),
        P(),
        P("rep"),
        P("rep"),
        P(("rep", "req"), None),
        P(),
    )
    out_specs = (P(("rep", "req"), None), P(("rep", "req"), None))
    return jax.shard_map(body, mesh=mesh, in_specs=in_specs, out_specs=out_specs, check_vma=False)
```
